32 devices in a mesh: seq: 8 (over z, x), tp: 4 (over y, core).
Axes of the slice: x: 2, y: 2, z: 4, core: 2. Of those that a mesh axis runs over, the one named last changes fastest.
Arguments:
- query_heads: bfloat16 [2048, 2048], P('seq', 'tp'), may hold values from -96 to 96
- key_heads: bfloat16 [2048, 2048], P('seq', 'tp'), may hold values from -4 to 4
- value_heads: bfloat16 [2048, 2048], P('seq', 'tp'), may hold values from -6 to 6
- residual: bfloat16 [2048, 4096], P('seq'), may hold values from -64 to 64
- out_weight: bfloat16 [2048, 4096], P('tp'), may hold values from -0.125 to 0.125
- ln_gain: float32 [4096], replicated, may hold values from 0.1 to 1.9
- up_source: bfloat16 [4096, 4096], P(None, 'tp'), may hold values from -0.09375 to 0.09375
- down_source: bfloat16 [4096, 4096], P('tp'), may hold values from -0.09375 to 0.09375
- copy_gain: float32 [4096], P('tp'), may hold values from 0.3 to 3
- neuron_source: int32 [4096], P('tp'), may hold values from 0 to 4095, as said below
- cotangent: bfloat16 [2048, 4096], P('seq'), may hold values from -6 to 6
Outputs:
- encoded: float32 [2048, 4096], P(('seq', 'tp'))
- grad_query: float32 [2048, 2048], P('seq', 'tp')
- grad_key: float32 [2048, 2048], P('seq', 'tp')
- grad_value: float32 [2048, 2048], P('seq', 'tp')
- grad_residual: float32 [2048, 4096], P('seq', 'tp')
The draws below stay inside these ranges and needn't reach their ends.
Inputs may be any that keep to these rules, and one draw needn't show every extreme that they name: Added neuron j splits a source neuron of its own group: neuron_source[j] // 1024 == j // 1024.
All inputs are finite; a program needn't handle non-finite values.
Results may differ from the reference program's by a relative error of at most 0.035.
Values may be sent and summed in bfloat16 or wider, within the bound.
A program may use at most 128 MiB of HBM per device.

```python
import math
import jax
import jax.numpy as jnp
from jax import lax

D = 4096
HEADS = 16
HEAD_DIM = 128
FF_SRC = 4096
FF_COPY = 4096
TOK_DEV = 256
TOKENS = 2048
SRC_SHARD = 1024
COPY_SHARD = 1024
N_SEQ = 8
N_TP = 4


def query_key_pair(key):
    head_width = HEADS * HEAD_DIM
    query_base = jax.random.truncated_normal(jax.random.fold_in(key, 11), -4.0, 4.0, (TOKENS, head_width), jnp.float32)
    key_base = jax.random.truncated_normal(jax.random.fold_in(key, 12), -4.0, 4.0, (TOKENS, head_width), jnp.float32)
    return (query_base, key_base)


def draw_query_heads(key, part):
    return query_key_pair(key)[0].astype(jnp.bfloat16)


def draw_key_heads(key, part):
    return query_key_pair(key)[1].astype(jnp.bfloat16)


def draw_residual(key, part):
    base = jax.random.truncated_normal(jax.random.fold_in(key, 21), -5.0, 5.0, (TOKENS, D), jnp.float32)
    column_scale = jnp.exp(jax.random.uniform(jax.random.fold_in(key, 22), (1, D), jnp.float32, math.log(0.3), math.log(3.0)))
    return (base * column_scale).astype(jnp.bfloat16)


def draw_neuron_source(key, part):
    local_pick = jax.random.randint(key, (FF_COPY,), 0, SRC_SHARD, dtype=jnp.int32)
    owner_group = jnp.arange(FF_COPY, dtype=jnp.int32) // COPY_SHARD
    picked = owner_group * SRC_SHARD + local_pick
    return picked.at[0].set(0).at[FF_COPY - 1].set(FF_SRC - 1)


def shard_levels(own_key, extent, pieces, low, largest):
    level = 1.0
    for position, parts in pieces:
        steps = jax.random.uniform(jax.random.fold_in(jax.random.fold_in(own_key, 6), position), (parts,), jnp.float32, low / len(pieces), largest / len(pieces))
        level = level * jnp.repeat(jnp.exp(steps), extent[position] // parts).reshape((-1,) + (1,) * (len(extent) - 1 - position))
    return level


def noise(own_key, dims, width, limit, cuts=(), held_as=jnp.bfloat16):
    values = jax.random.normal(own_key, dims, jnp.float32) * width
    if len(cuts) > 0:
        values = shard_levels(own_key, dims, cuts, -0.22, 0.18) * values
    return jnp.clip(values, min=-limit, max=limit).astype(held_as)


def setup_inputs(seed: int = 0) -> dict:
    seeds = jax.random.split(jax.random.key(seed), 12)
    query_heads = draw_query_heads(jax.random.fold_in(seeds[11], 71), 0)
    key_heads = draw_key_heads(jax.random.fold_in(seeds[11], 71), 0)
    value_heads = noise(seeds[2], (TOKENS, HEADS * HEAD_DIM), 1.0, 6.0, ((0, 8), (1, 4)))
    residual = draw_residual(jax.random.fold_in(seeds[11], 71), 0)
    out_weight = noise(seeds[4], (HEADS * HEAD_DIM, D), (HEADS * HEAD_DIM) ** -0.5, 0.125, ((0, 4),))
    ln_gain = jnp.clip(1.0 + 0.18 * jax.random.normal(seeds[5], (D,), jnp.float32), 0.1, 1.9)
    up_source = noise(seeds[6], (D, FF_SRC), D ** -0.5, 0.09375, ((1, 4),))
    down_source = noise(seeds[7], (FF_SRC, D), FF_SRC ** -0.5, 0.09375, ((0, 4),))
    copy_gain = jnp.clip(jnp.exp(math.log(3.0) - 2.3025851 * jax.random.uniform(seeds[8], (FF_COPY,), jnp.float32) ** shard_levels(seeds[8], (FF_COPY,), ((0, 4),), -0.2, 0.2)), 0.3, 3.0)
    neuron_source = draw_neuron_source(jax.random.fold_in(seeds[11], 71), 0)
    cotangent = noise(seeds[10], (TOKENS, D), 1.0, 6.0, ((0, 8),))
    return dict(query_heads=query_heads, key_heads=key_heads, value_heads=value_heads, residual=residual, out_weight=out_weight, ln_gain=ln_gain, up_source=up_source, down_source=down_source, copy_gain=copy_gain, neuron_source=neuron_source, cotangent=cotangent)


epsilon = 1e-05

def gelu_slope(inputs):
    output, pull_back = jax.vjp(jax.nn.gelu, inputs)
    return (output, pull_back(jnp.ones_like(inputs))[0])

def layer_norm_rows(stream):
    centered = stream - lax.optimization_barrier(jnp.mean(stream, axis=-1, keepdims=True))
    row_sigma = jnp.sqrt(lax.optimization_barrier(jnp.mean(centered * centered, axis=-1, keepdims=True)) + epsilon)
    return (centered / row_sigma, row_sigma)

def reference(query_heads, key_heads, value_heads, residual, out_weight, ln_gain, up_source, down_source, copy_gain, neuron_source, cotangent):
    head_width = HEADS * HEAD_DIM
    group_heads = head_width // N_TP
    group_src = FF_SRC // N_TP
    score_scale = 1.0 / math.sqrt(HEAD_DIM)
    margin = 2 * TOK_DEV
    span_rows = 5 * TOK_DEV

    def pad_rows(array):
        return jnp.pad(array.reshape(TOKENS, HEADS, HEAD_DIM), ((margin, margin), (0, 0), (0, 0)))
    key_pad = pad_rows(key_heads)
    value_pad = pad_rows(value_heads)

    def block_view(block):
        row_start = (block * TOK_DEV).astype(jnp.int32)
        queries = lax.dynamic_slice_in_dim(query_heads, row_start, TOK_DEV, 0).reshape(TOK_DEV, HEADS, HEAD_DIM)
        keys_near = lax.dynamic_slice_in_dim(key_pad, row_start, span_rows, 0)
        values_near = lax.dynamic_slice_in_dim(value_pad, row_start, span_rows, 0)
        block_of = block + jnp.arange(span_rows, dtype=jnp.int32) // TOK_DEV - 2
        is_valid = (block_of >= 0) & (block_of < N_SEQ)
        scores = jnp.einsum('rhd,khd->hrk', queries.astype(jnp.float32), keys_near.astype(jnp.float32)) * score_scale
        scores = jnp.where(is_valid[None, None, :], scores, -jnp.inf)
        row_top = lax.optimization_barrier(jnp.max(scores, axis=-1, keepdims=True))
        exp_scores = jnp.exp(scores - row_top)
        attn_probs = exp_scores / lax.optimization_barrier(jnp.sum(exp_scores, axis=-1, keepdims=True))
        return (row_start, queries, keys_near, values_near, attn_probs)

    def forward_block(block):
        row_start, queries, keys_near, values_near, attn_probs = block_view(block)
        attn_low = attn_probs.astype(jnp.bfloat16)
        return jnp.einsum('hrk,khd->rhd', attn_low.astype(jnp.float32), values_near.astype(jnp.float32)).astype(jnp.bfloat16)
    block_ids = jnp.arange(N_SEQ, dtype=jnp.int32)
    attended = lax.map(forward_block, block_ids).reshape(TOKENS, head_width)
    mixed = jnp.zeros((TOKENS, D), jnp.float32)
    for group_index in range(N_TP):
        head_cols = slice(group_index * group_heads, (group_index + 1) * group_heads)
        head_part = jnp.dot(attended[:, head_cols], out_weight[head_cols], preferred_element_type=jnp.float32).astype(jnp.bfloat16)
        mixed = mixed + head_part.astype(jnp.float32)
    stream = residual.astype(jnp.float32) + mixed
    unit_rows, row_sigma = layer_norm_rows(stream)
    normed_full = unit_rows * ln_gain
    normed = normed_full.astype(jnp.bfloat16)
    hidden_in = jnp.dot(normed, up_source, preferred_element_type=jnp.float32)
    counts = jnp.ones((FF_SRC,), jnp.float32).at[neuron_source].add(1.0)
    copies_in = hidden_in[:, neuron_source] * copy_gain
    act_src, slope_src = gelu_slope(hidden_in)
    act_copy, slope_copy = gelu_slope(copies_in)
    merged = (act_src.at[:, neuron_source].add(act_copy) / counts).astype(jnp.bfloat16)
    ffn_total = jnp.zeros((TOKENS, D), jnp.float32)
    for group_index in range(N_TP):
        src_cols = slice(group_index * group_src, (group_index + 1) * group_src)
        ffn_part = jnp.dot(merged[:, src_cols], down_source[src_cols], preferred_element_type=jnp.float32).astype(jnp.bfloat16)
        ffn_total = ffn_total + ffn_part.astype(jnp.float32)
    encoded = normed_full + ffn_total
    grad_merged = jnp.dot(cotangent, down_source.T, preferred_element_type=jnp.float32)
    inverse = 1.0 / counts
    grad_src = grad_merged * inverse * slope_src
    grad_copy = grad_merged[:, neuron_source] * inverse[neuron_source] * slope_copy
    grad_hidden = grad_src.at[:, neuron_source].add(grad_copy * copy_gain).astype(jnp.bfloat16)
    grad_normed = cotangent.astype(jnp.float32)
    for group_index in range(N_TP):
        src_cols = slice(group_index * group_src, (group_index + 1) * group_src)
        back_part = jnp.dot(grad_hidden[:, src_cols], up_source[:, src_cols].T, preferred_element_type=jnp.float32).astype(jnp.bfloat16)
        grad_normed = grad_normed + back_part.astype(jnp.float32)
    scaled = grad_normed * ln_gain
    grad_residual = (scaled - lax.optimization_barrier(jnp.mean(scaled, axis=-1, keepdims=True)) - unit_rows * lax.optimization_barrier(jnp.mean(scaled * unit_rows, axis=-1, keepdims=True))) / row_sigma
    grad_low = grad_residual.astype(jnp.bfloat16)
    grad_attended = jnp.dot(grad_low, out_weight.T, preferred_element_type=jnp.float32).astype(jnp.bfloat16)
    grad_start = jnp.zeros((TOKENS + 2 * margin, HEADS, HEAD_DIM), jnp.float32)

    def backward_block(carry, block):
        key_acc, value_acc = carry
        row_start, queries, keys_near, values_near, attn_probs = block_view(block)
        attn_low = attn_probs.astype(jnp.bfloat16)
        out_block = lax.dynamic_slice_in_dim(attended, row_start, TOK_DEV, 0).reshape(TOK_DEV, HEADS, HEAD_DIM)
        grad_block = lax.dynamic_slice_in_dim(grad_attended, row_start, TOK_DEV, 0).reshape(TOK_DEV, HEADS, HEAD_DIM)
        row_delta = lax.optimization_barrier(jnp.sum(grad_block.astype(jnp.float32) * out_block.astype(jnp.float32), axis=-1)).T
        grad_probs = jnp.einsum('rhd,khd->hrk', grad_block.astype(jnp.float32), values_near.astype(jnp.float32))
        grad_scores = (attn_probs * (grad_probs - row_delta[:, :, None])).astype(jnp.bfloat16)
        grad_q = score_scale * jnp.einsum('hrk,khd->rhd', grad_scores.astype(jnp.float32), keys_near.astype(jnp.float32))
        grad_k = score_scale * jnp.einsum('hrk,rhd->khd', grad_scores.astype(jnp.float32), queries.astype(jnp.float32))
        grad_v = jnp.einsum('hrk,rhd->khd', attn_low.astype(jnp.float32), grad_block.astype(jnp.float32))
        key_acc = lax.dynamic_update_slice_in_dim(key_acc, lax.dynamic_slice_in_dim(key_acc, row_start, span_rows, 0) + grad_k, row_start, 0)
        value_acc = lax.dynamic_update_slice_in_dim(value_acc, lax.dynamic_slice_in_dim(value_acc, row_start, span_rows, 0) + grad_v, row_start, 0)
        return ((key_acc, value_acc), grad_q)
    (key_acc, value_acc), grad_q = lax.scan(backward_block, (grad_start, grad_start), block_ids)
    grad_query = grad_q.reshape(TOKENS, head_width)
    grad_key = key_acc[margin:margin + TOKENS].reshape(TOKENS, head_width)
    grad_value = value_acc[margin:margin + TOKENS].reshape(TOKENS, head_width)
    return (encoded, grad_query, grad_key, grad_value, grad_residual)
```

```python
import math

import jax
import jax.numpy as jnp
from jax import lax
from jax.sharding import PartitionSpec as P

HEAD_DIM = 128


epsilon = 1e-05


def from_behind(array, axis, by):
    count = lax.axis_size(axis)
    pairs = [(i, i + by) for i in range(count) if 0 <= i + by < count]
    return lax.ppermute(array, axis, pairs)


def gelu_slope(inputs):
    output, pull_back = jax.vjp(jax.nn.gelu, inputs)
    return (output, pull_back(jnp.ones_like(inputs))[0])


def layer_norm_rows(stream):
    centered = stream - jnp.mean(stream, axis=-1, keepdims=True)
    row_sigma = jnp.sqrt(jnp.mean(centered * centered, axis=-1, keepdims=True) + epsilon)
    return (centered / row_sigma, row_sigma)


def bfloat16_term(values):
    return lax.optimization_barrier(values.astype(jnp.bfloat16)).astype(jnp.float32)


def shards(
    query_heads,
    key_heads,
    value_heads,
    residual,
    out_weight,
    ln_gain,
    up_source,
    down_source,
    copy_gain,
    neuron_source,
    cotangent,
):
    tok_rows = query_heads.shape[0]
    head_width = query_heads.shape[1]
    head_count = head_width // HEAD_DIM
    model_width = residual.shape[1]
    score_scale = 1.0 / math.sqrt(HEAD_DIM)
    cycle_place = lax.axis_index("seq")
    blocks = lax.axis_size("seq")
    tp_place = lax.axis_index("tp")
    groups = lax.axis_size("tp")
    kv_pair = jnp.stack([key_heads, value_heads])
    kv_blocks = {0: kv_pair}
    for offset in (-2, -1, 1, 2):
        kv_blocks[offset] = from_behind(kv_pair, "seq", -offset)
    window = jnp.concatenate([kv_blocks[offset] for offset in (-2, -1, 0, 1, 2)], axis=1)
    keys_all = window[0].reshape(5 * tok_rows, head_count, HEAD_DIM)
    values_all = window[1].reshape(5 * tok_rows, head_count, HEAD_DIM)
    block_of = jnp.arange(5 * tok_rows, dtype=jnp.int32) // tok_rows - 2 + cycle_place
    is_valid = (block_of >= 0) & (block_of < blocks)
    queries = query_heads.reshape(tok_rows, head_count, HEAD_DIM)
    scores = (
        jnp.einsum("rhd,khd->hrk", queries, keys_all, preferred_element_type=jnp.float32)
        * score_scale
    )
    scores = jnp.where(is_valid[None, None, :], scores, -jnp.inf)
    row_top = jnp.max(scores, axis=-1, keepdims=True)
    exp_scores = jnp.exp(scores - row_top)
    attn_probs = exp_scores / jnp.sum(exp_scores, axis=-1, keepdims=True)
    attn_low = attn_probs.astype(jnp.bfloat16)
    attended = jnp.einsum(
        "hrk,khd->rhd", attn_low, values_all, preferred_element_type=jnp.float32
    ).astype(jnp.bfloat16)
    attended = attended.reshape(tok_rows, head_width)
    head_part = bfloat16_term(jnp.dot(attended, out_weight, preferred_element_type=jnp.float32))
    head_mix = lax.psum(head_part.astype(jnp.bfloat16), "tp").astype(jnp.float32)
    stream = residual.astype(jnp.float32) + head_mix
    unit_rows, row_sigma = layer_norm_rows(stream)
    normed_full = unit_rows * ln_gain
    normed = normed_full.astype(jnp.bfloat16)
    src_width = up_source.shape[1]
    local_source = neuron_source - tp_place * src_width
    pick = (lax.broadcasted_iota(jnp.int32, (src_width, local_source.shape[0]), 0) == local_source[None, :])
    counts = 1.0 + jnp.sum(pick.astype(jnp.float32), axis=1)
    pick = pick.astype(jnp.bfloat16)

    def copies_of(values):
        return jnp.dot(values.astype(jnp.bfloat16), pick, preferred_element_type=jnp.float32)

    def summed(values):
        return lax.dot_general(
            values.astype(jnp.bfloat16), pick, (((1,), (1,)), ((), ())), preferred_element_type=jnp.float32
        )

    hidden_in = jnp.dot(normed, up_source, preferred_element_type=jnp.float32)
    copies_in = copies_of(hidden_in) * copy_gain
    act_src, slope_src = gelu_slope(hidden_in)
    act_copy, slope_copy = gelu_slope(copies_in)
    merged = ((act_src + summed(act_copy)) / counts).astype(jnp.bfloat16)
    owner_rows = tok_rows // groups
    ffn_out = lax.psum_scatter(
        bfloat16_term(jnp.dot(merged, down_source, preferred_element_type=jnp.float32)).astype(
            jnp.bfloat16
        ),
        "tp",
        scatter_dimension=0,
        tiled=True,
    ).astype(jnp.float32)
    own_normed = lax.dynamic_slice_in_dim(normed_full, tp_place * owner_rows, owner_rows, 0)
    encoded = own_normed + ffn_out
    grad_merged = lax.dot_general(
        cotangent, down_source, (((1,), (1,)), ((), ())), preferred_element_type=jnp.float32
    )
    inverse = 1.0 / counts
    grad_src = grad_merged * inverse * slope_src
    grad_copy = copies_of(grad_merged * inverse) * slope_copy
    grad_hidden = (grad_src + summed(grad_copy * copy_gain)).astype(jnp.bfloat16)
    back_part = bfloat16_term(
        lax.dot_general(
            grad_hidden, up_source, (((1,), (1,)), ((), ())), preferred_element_type=jnp.float32
        )
    )
    grad_normed = cotangent.astype(jnp.float32) + lax.psum(
        back_part.astype(jnp.bfloat16), "tp"
    ).astype(jnp.float32)
    scaled = grad_normed * ln_gain
    grad_stream = (
        scaled
        - jnp.mean(scaled, axis=-1, keepdims=True)
        - unit_rows * jnp.mean(scaled * unit_rows, axis=-1, keepdims=True)
    ) / row_sigma
    grad_low = grad_stream.astype(jnp.bfloat16)
    col_width = model_width // groups
    grad_residual = lax.dynamic_slice_in_dim(grad_stream, tp_place * col_width, col_width, 1)
    grad_attended = lax.dot_general(
        grad_low, out_weight, (((1,), (1,)), ((), ())), preferred_element_type=jnp.float32
    ).astype(jnp.bfloat16)
    grad_heads = grad_attended.reshape(tok_rows, head_count, HEAD_DIM)
    attended_heads = attended.reshape(tok_rows, head_count, HEAD_DIM)
    row_delta = jnp.sum(
        grad_heads.astype(jnp.float32) * attended_heads.astype(jnp.float32), axis=-1
    ).T
    grad_probs = jnp.einsum(
        "rhd,khd->hrk", grad_heads, values_all, preferred_element_type=jnp.float32
    )
    grad_scores = (attn_probs * (grad_probs - row_delta[:, :, None])).astype(jnp.bfloat16)
    grad_query = score_scale * jnp.einsum(
        "hrk,khd->rhd", grad_scores, keys_all, preferred_element_type=jnp.float32
    )
    grad_query = grad_query.reshape(tok_rows, head_width)
    grad_keys = score_scale * jnp.einsum(
        "hrk,rhd->khd", grad_scores, queries, preferred_element_type=jnp.float32
    )
    grad_values = jnp.einsum(
        "hrk,rhd->khd", attn_low, grad_heads, preferred_element_type=jnp.float32
    )
    partial_value = jnp.stack(
        [grad_keys.reshape(5 * tok_rows, head_width), grad_values.reshape(5 * tok_rows, head_width)]
    )
    pieces = {}
    for offset in (-2, -1, 0, 1, 2):
        pieces[offset] = partial_value[:, (offset + 2) * tok_rows : (offset + 3) * tok_rows]
    grad_total = pieces[0]
    for offset in (-2, -1, 1, 2):
        grad_total = grad_total + from_behind(pieces[offset].astype(jnp.bfloat16), "seq", offset).astype(jnp.float32)
    grad_key = grad_total[0]
    grad_value = grad_total[1]
    return (encoded, grad_query, grad_key, grad_value, grad_residual)


def solution(mesh):
    in_specs = (
        P("seq", "tp"),
        P("seq", "tp"),
        P("seq", "tp"),
        P("seq", None),
        P("tp", None),
        P(),
        P(None, "tp"),
        P("tp", None),
        P("tp"),
        P("tp"),
        P("seq", None),
    )
    out_specs = (
        P(("seq", "tp"), None),
        P("seq", "tp"),
        P("seq", "tp"),
        P("seq", "tp"),
        P("seq", "tp"),
    )
    return jax.shard_map(shards, mesh=mesh, in_specs=in_specs, out_specs=out_specs, check_vma=False)
```

```python
import functools
import math

import jax
import jax.numpy as jnp
from jax import lax
from jax.experimental import pallas as pl
from jax.experimental.pallas import tpu as pltpu
from jax.sharding import PartitionSpec as P

HEAD_DIM = 128
OFFSETS = (-2, -1, 1, 2)
CHUNKS = 2
TILE = 512
epsilon = 1e-05
MESH = pl.DeviceIdType.MESH
VM = pltpu.VMEM
F32 = jnp.float32
BF16 = jnp.bfloat16
SCALE = 1.0 / math.sqrt(HEAD_DIM)


def dot_nn(a, b):
    return jnp.dot(a, b, preferred_element_type=F32)


def dot_nt(a, b):
    return lax.dot_general(a, b, (((1,), (1,)), ((), ())), preferred_element_type=F32)


def dot_tn(a, b):
    return lax.dot_general(a, b, (((0,), (0,)), ((), ())), preferred_element_type=F32)


def remote(src, dst, send, recv, **where):
    return pltpu.make_async_remote_copy(
        src_ref=src, dst_ref=dst, send_sem=send, recv_sem=recv, device_id=where, device_id_type=MESH
    )


class Blocks:
    def __init__(self, count):
        self.count = count
        self.place = lax.axis_index("seq")

    def there(self, offset):
        other = self.place + offset
        return (other >= 0) & (other < self.count)

    def greet(self, barrier):
        for offset in OFFSETS:
            @pl.when(self.there(offset))
            def _():
                pl.semaphore_signal(
                    barrier, inc=1, device_id={"seq": self.place + offset}, device_id_type=MESH
                )

    def greeted(self, barrier, more=0):
        peers = sum(self.there(offset).astype(jnp.int32) for offset in OFFSETS)
        pl.semaphore_wait(barrier, peers + more)

    def copy(self, src, window, send, recv, to, slot, sent):
        return remote(src, window.at[slot], send.at[sent], recv.at[slot], seq=self.place + to)

    def send(self, src, window, send, recv):
        for index, offset in enumerate(OFFSETS):
            @pl.when(self.there(offset))
            def _():
                self.copy(src, window, send, recv, offset, 3 - index, index).start()

    def clear(self, window):
        for index, offset in enumerate(OFFSETS):
            @pl.when(jnp.logical_not(self.there(offset)))
            def _():
                window[index] = jnp.zeros(window.shape[1:], window.dtype)

    def arrive(self, src, window, send, recv, index):
        offset = OFFSETS[index]
        @pl.when(self.there(offset))
        def _():
            self.copy(src, window, send, recv, offset, index, index).wait_recv()

    def left(self, src, window, send, recv):
        for index, offset in enumerate(OFFSETS):
            @pl.when(self.there(offset))
            def _():
                self.copy(src, window, send, recv, offset, 3 - index, index).wait_send()


class Group:
    def __init__(self):
        me = lax.axis_index("tp")
        chip, core = lax.div(me, 2), lax.rem(me, 2)
        self.me = me
        self.sibling = chip * 2 + 1 - core
        self.far = (1 - chip) * 2 + core
        self.across = (1 - chip) * 2 + 1 - core

    def greet(self, barrier):
        for other in (self.sibling, self.far):
            pl.semaphore_signal(barrier, inc=1, device_id={"tp": other}, device_id_type=MESH)


def attend_kernel(
    count, q_ref, k_ref, v_ref, out_ref, kwin, vwin, stat_ref, prob, ks, kr, vs, vr
):
    blocks = Blocks(count)
    barrier = pltpu.get_barrier_semaphore()
    blocks.greet(barrier)
    blocks.greeted(barrier)
    blocks.send(k_ref, kwin, ks, kr)
    blocks.send(v_ref, vwin, vs, vr)
    blocks.clear(kwin)
    blocks.clear(vwin)
    rows, width = q_ref.shape
    heads = width // HEAD_DIM
    for index in range(4):
        blocks.arrive(k_ref, kwin, ks, kr, index)
    bias = [jnp.where(blocks.there(offset), 0.0, -1e30).astype(F32) for offset in OFFSETS]
    lane = lax.broadcasted_iota(jnp.int32, (rows, 128), 1)
    stats = jnp.zeros((rows, 128), F32)
    for h in range(heads):
        cols = slice(h * HEAD_DIM, (h + 1) * HEAD_DIM)
        qh = q_ref[:, cols]
        scores = [dot_nt(qh, k_ref[:, cols]) * SCALE]
        for index in range(4):
            scores.append(dot_nt(qh, kwin[index, :, cols]) * SCALE + bias[index])
        top = scores[0]
        for s in scores[1:]:
            top = jnp.maximum(top, s)
        top = jnp.max(top, axis=1, keepdims=True)
        exps = [jnp.exp(s - top) for s in scores]
        total = exps[0]
        for e in exps[1:]:
            total = total + e
        inverse = 1.0 / jnp.sum(total, axis=1, keepdims=True)
        for index in range(5):
            prob[h, index] = (exps[index] * inverse).astype(BF16)
        stats = jnp.where(lane == h, top, stats)
        stats = jnp.where(lane == heads + h, inverse, stats)
    stat_ref[...] = jnp.transpose(stats)[: 2 * heads]
    for index in range(4):
        blocks.arrive(v_ref, vwin, vs, vr, index)
    for h in range(heads):
        cols = slice(h * HEAD_DIM, (h + 1) * HEAD_DIM)
        acc = dot_nn(prob[h, 0], v_ref[:, cols])
        for index in range(4):
            acc = acc + dot_nn(prob[h, index + 1], vwin[index, :, cols])
        out_ref[:, cols] = acc.astype(BF16)
    blocks.left(k_ref, kwin, ks, kr)
    blocks.left(v_ref, vwin, vs, vr)


def attend(count, q, k, v):
    rows, width = q.shape
    heads = width // HEAD_DIM
    win = jax.ShapeDtypeStruct((4, rows, width), BF16)
    dma = pltpu.SemaphoreType.DMA((4,))
    return pl.pallas_call(
        functools.partial(attend_kernel, count),
        out_shape=(
            jax.ShapeDtypeStruct((rows, width), BF16),
            win,
            win,
            jax.ShapeDtypeStruct((2 * heads, rows), F32),
        ),
        in_specs=[pl.BlockSpec(memory_space=VM)] * 3,
        out_specs=(pl.BlockSpec(memory_space=VM),) * 4,
        scratch_shapes=[VM((heads, 5, rows, rows), BF16), dma, dma, dma, dma],
        compiler_params=pltpu.CompilerParams(
            collective_id=1, has_side_effects=True, vmem_limit_bytes=32 << 20
        ),
        name="attend",
    )(q, k, v)


def reduce_first(group, own, part, mine, sbuf1, rbuf1, s1, r1):
    part((group.across, group.sibling), sbuf1)
    copies = [
        remote(sbuf1.at[i], rbuf1.at[i], s1.at[i], r1.at[i], tp=group.sibling) for i in range(2)
    ]
    for copy in copies:
        copy.start()
    part((group.far, group.me), mine)
    return copies


def reduce_second(group, own, mine, rbuf1, sbuf2, rbuf2, s2, r2, copies):
    copies[0].wait_recv()
    rows = own // CHUNKS
    out = []
    for ch in range(CHUNKS):
        sl = slice(ch * rows, (ch + 1) * rows)
        sbuf2[ch] = (mine[0, sl].astype(F32) + rbuf1[0, sl].astype(F32)).astype(BF16)
        copy = remote(sbuf2.at[ch], rbuf2.at[ch], s2.at[ch], r2.at[ch], tp=group.far)
        copy.start()
        out.append(copy)
    copies[1].wait_recv()
    return out


def spread(group, own, full, finish, seconds, ags, agr):
    rows = own // CHUNKS

    def at(owner, ch):
        return full.at[pl.ds(pl.multiple_of(owner * own + ch * rows, rows), rows)]

    to_sib, to_far, passed = [], [], []
    for ch in range(CHUNKS):
        seconds[ch].wait_recv()
        finish(ch, at(group.me, ch))
        mine = at(group.me, ch)
        to_far.append(remote(mine, mine, ags.at[ch, 0], agr.at[ch, 0], tp=group.far))
        to_far[ch].start()
        to_sib.append(remote(mine, mine, ags.at[ch, 1], agr.at[ch, 1], tp=group.sibling))
        to_sib[ch].start()
    for ch in range(CHUNKS):
        to_far[ch].wait_recv()
        got = at(group.far, ch)
        passed.append(remote(got, got, ags.at[ch, 2], agr.at[ch, 2], tp=group.sibling))
        passed[ch].start()
    for ch in range(CHUNKS):
        to_sib[ch].wait_recv()
        passed[ch].wait_recv()
    return to_sib + to_far + passed


def norm_kernel(
    count, att_ref, w_ref, res_ref, gain_ref, q_ref, stat_ref,
    full, unit_ref, sigma_ref, qwin, swin,
    mine, sbuf1, rbuf1, sbuf2, rbuf2, res_buf,
    s1, r1, s2, r2, ags, agr, qs, qr, ss, sr, res_sem,
):
    blocks, group = Blocks(count), Group()
    own, width = unit_ref.shape
    rows = own // CHUNKS
    fetch = pltpu.make_async_copy(
        res_ref.at[pl.ds(pl.multiple_of(group.me * own, own), own)], res_buf, res_sem
    )
    fetch.start()
    barrier = pltpu.get_barrier_semaphore()
    group.greet(barrier)
    blocks.greet(barrier)
    blocks.greeted(barrier, 2)
    blocks.send(q_ref, qwin, qs, qr)
    blocks.send(stat_ref, swin, ss, sr)

    def part(owners, dst):
        lhs = jnp.concatenate(
            [att_ref[pl.ds(pl.multiple_of(o * own, own), own), :] for o in owners], axis=0
        )

        @pl.loop(0, width // TILE)
        def _(ct):
            cols = pl.ds(pl.multiple_of(ct * TILE, TILE), TILE)
            r = dot_nn(lhs, w_ref[:, cols]).astype(BF16)
            dst[0, :, cols] = r[:own]
            dst[1, :, cols] = r[own:]

    firsts = reduce_first(group, own, part, mine, sbuf1, rbuf1, s1, r1)
    blocks.clear(qwin)
    blocks.clear(swin)
    seconds = reduce_second(group, own, mine, rbuf1, sbuf2, rbuf2, s2, r2, firsts)
    fetch.wait()

    def finish(ch, dst):
        sl = slice(ch * rows, (ch + 1) * rows)
        stream = (
            res_buf[sl].astype(F32)
            + mine[1, sl].astype(F32)
            + rbuf1[1, sl].astype(F32)
            + rbuf2[ch].astype(F32)
        )
        centered = stream - jnp.mean(stream, axis=1, keepdims=True)
        sigma = jnp.sqrt(jnp.mean(centered * centered, axis=1, keepdims=True) + epsilon)
        unit = centered / sigma
        unit_ref[sl] = unit
        sigma_ref[sl] = jnp.broadcast_to(sigma, (rows, 128))
        dst[...] = (unit * gain_ref[...]).astype(BF16)

    tails = spread(group, own, full, finish, seconds, ags, agr)
    for copy in firsts + seconds + tails:
        copy.wait_send()
    for index in range(4):
        blocks.arrive(q_ref, qwin, qs, qr, index)
        blocks.arrive(stat_ref, swin, ss, sr, index)
    blocks.left(q_ref, qwin, qs, qr)
    blocks.left(stat_ref, swin, ss, sr)


def reduce_scratch(own, width):
    two = VM((2, own, width), BF16)
    chunk = VM((CHUNKS, own // CHUNKS, width), BF16)
    return [two, two, two, chunk, chunk]


def reduce_sems():
    dma = pltpu.SemaphoreType.DMA
    return [dma((2,)), dma((2,)), dma((CHUNKS,)), dma((CHUNKS,))]


def norm_stage(count, groups, att, w, residual, gain, q, stats):
    tok, width = residual.shape
    own = tok // groups
    dma = pltpu.SemaphoreType.DMA
    vm = pl.BlockSpec(memory_space=VM)
    return pl.pallas_call(
        functools.partial(norm_kernel, count),
        out_shape=(
            jax.ShapeDtypeStruct((tok, width), BF16),
            jax.ShapeDtypeStruct((own, width), F32),
            jax.ShapeDtypeStruct((own, 128), F32),
            jax.ShapeDtypeStruct((4,) + q.shape, BF16),
            jax.ShapeDtypeStruct((4,) + stats.shape, F32),
        ),
        in_specs=[vm, vm, pl.BlockSpec(memory_space=pl.ANY), vm, vm, vm],
        out_specs=(vm,) * 5,
        scratch_shapes=reduce_scratch(own, width)
        + [VM((own, width), BF16)]
        + reduce_sems()
        + [dma((CHUNKS, 3)), dma((CHUNKS, 3))]
        + [dma((4,))] * 4
        + [dma(())],
        compiler_params=pltpu.CompilerParams(
            collective_id=2, has_side_effects=True, vmem_limit_bytes=40 << 20
        ),
        name="norm_stage",
    )(att, w, residual, gain, q, stats)


def back_kernel(
    gh_ref, w_ref, cot_ref, gain_ref, unit_ref, sigma_ref,
    full,
    mine, sbuf1, rbuf1, sbuf2, rbuf2, cot_buf,
    s1, r1, s2, r2, ags, agr, cot_sem,
):
    group = Group()
    own, width = unit_ref.shape
    rows = own // CHUNKS
    fetch = pltpu.make_async_copy(
        cot_ref.at[pl.ds(pl.multiple_of(group.me * own, own), own)], cot_buf, cot_sem
    )
    fetch.start()
    barrier = pltpu.get_barrier_semaphore()
    group.greet(barrier)
    pl.semaphore_wait(barrier, 2)

    def part(owners, dst):
        lhs = jnp.concatenate(
            [gh_ref[pl.ds(pl.multiple_of(o * own, own), own), :] for o in owners], axis=0
        )

        @pl.loop(0, width // TILE)
        def _(ct):
            cols = pl.ds(pl.multiple_of(ct * TILE, TILE), TILE)
            r = dot_nt(lhs, w_ref[cols, :]).astype(BF16)
            dst[0, :, cols] = r[:own]
            dst[1, :, cols] = r[own:]

    firsts = reduce_first(group, own, part, mine, sbuf1, rbuf1, s1, r1)
    seconds = reduce_second(group, own, mine, rbuf1, sbuf2, rbuf2, s2, r2, firsts)
    fetch.wait()

    def finish(ch, dst):
        sl = slice(ch * rows, (ch + 1) * rows)
        grad = (
            cot_buf[sl].astype(F32)
            + mine[1, sl].astype(F32)
            + rbuf1[1, sl].astype(F32)
            + rbuf2[ch].astype(F32)
        )
        scaled = grad * gain_ref[...]
        unit = unit_ref[sl]
        mean = jnp.mean(scaled, axis=1, keepdims=True)
        along = jnp.mean(scaled * unit, axis=1, keepdims=True)
        dst[...] = ((scaled - mean - unit * along) / sigma_ref[sl, :1]).astype(BF16)

    tails = spread(group, own, full, finish, seconds, ags, agr)
    for copy in firsts + seconds + tails:
        copy.wait_send()


def back_stage(groups, gh, w, cotangent, gain, unit, sigma):
    tok, width = cotangent.shape
    own = tok // groups
    dma = pltpu.SemaphoreType.DMA
    vm = pl.BlockSpec(memory_space=VM)
    return pl.pallas_call(
        back_kernel,
        out_shape=jax.ShapeDtypeStruct((tok, width), BF16),
        in_specs=[vm, vm, pl.BlockSpec(memory_space=pl.ANY), vm, vm, vm],
        out_specs=vm,
        scratch_shapes=reduce_scratch(own, width)
        + [VM((own, width), BF16)]
        + reduce_sems()
        + [dma((CHUNKS, 3)), dma((CHUNKS, 3)), dma(())],
        compiler_params=pltpu.CompilerParams(
            collective_id=3, has_side_effects=True, vmem_limit_bytes=40 << 20
        ),
        name="back_stage",
    )(gh, w, cotangent, gain, unit, sigma)


def grads_kernel(
    count, low_ref, w_ref, att_ref, q_ref, k_ref, v_ref, kwin, vwin, qwin, stat_ref, swin,
    ffn_ref, unit_ref, gain_ref,
    enc_ref, gq_ref, gk_ref, gv_ref,
    dwin, twin, do_ref, delta_ref, rbuf1, sbuf2, rbuf2,
    ds_, dr, ts, tr, s1, r1, s2, r2,
):
    blocks, group = Blocks(count), Group()
    own, width = unit_ref.shape
    tok, cols_all = q_ref.shape
    heads = cols_all // HEAD_DIM
    rows = own // CHUNKS
    barrier = pltpu.get_barrier_semaphore()
    group.greet(barrier)
    blocks.greet(barrier)
    blocks.greeted(barrier, 2)

    def ffn_rows(owner):
        return ffn_ref.at[pl.ds(pl.multiple_of(owner * own, own), own)]

    firsts = [
        remote(ffn_rows(owner), rbuf1.at[i], s1.at[i], r1.at[i], tp=group.sibling)
        for i, owner in enumerate((group.across, group.sibling))
    ]
    for copy in firsts:
        copy.start()
    lane = lax.broadcasted_iota(jnp.int32, (tok, 128), 1)
    grad_att = dot_nt(low_ref[...], w_ref[...]).astype(BF16)
    do_ref[...] = grad_att
    blocks.send(do_ref, dwin, ds_, dr)
    deltas = jnp.zeros((tok, 128), F32)
    for h in range(heads):
        cols = slice(h * HEAD_DIM, (h + 1) * HEAD_DIM)
        delta = jnp.sum(
            grad_att[:, cols].astype(F32) * att_ref[:, cols].astype(F32), axis=1, keepdims=True
        )
        deltas = jnp.where(lane == h, delta, deltas)
    delta_ref[...] = jnp.transpose(deltas)[:8]
    blocks.send(delta_ref, twin, ts, tr)
    blocks.clear(dwin)
    blocks.clear(twin)
    firsts[0].wait_recv()
    seconds = []
    far_rows = ffn_rows(group.far)
    for ch in range(CHUNKS):
        sl = slice(ch * rows, (ch + 1) * rows)
        sbuf2[ch] = (far_rows[sl].astype(F32) + rbuf1[0, sl].astype(F32)).astype(BF16)
        seconds.append(remote(sbuf2.at[ch], rbuf2.at[ch], s2.at[ch], r2.at[ch], tp=group.far))
        seconds[ch].start()

    def pair(queries, keys, values, grads, stats, delta_row, h):
        top = stats[pl.ds(h, 1), :]
        inverse = stats[pl.ds(heads + h, 1), :]
        prob = jnp.exp(dot_nt(keys, queries) * SCALE - top) * inverse
        slope = (prob * (dot_nt(values, grads) - delta_row[pl.ds(h, 1), :])).astype(BF16)
        return prob.astype(BF16), slope

    @pl.loop(0, heads)
    def _(h):
        cols = pl.ds(pl.multiple_of(h * HEAD_DIM, HEAD_DIM), HEAD_DIM)
        qh, gh = q_ref[:, cols], do_ref[:, cols]
        kh, vh = k_ref[:, cols], v_ref[:, cols]
        prob, slope = pair(qh, kh, vh, gh, stat_ref, delta_ref, h)
        gv_ref[:, cols] = dot_nn(prob, gh)
        gk_ref[:, cols] = dot_nn(slope, qh)
        acc = dot_tn(slope, kh)
        for index in range(4):
            k_off, v_off = kwin[index, :, cols], vwin[index, :, cols]
            live = jnp.where(blocks.there(OFFSETS[index]), 1.0, 0.0).astype(F32)
            _, slope = pair_off(qh, k_off, v_off, gh, stat_ref, delta_ref, h, live)
            acc = acc + dot_tn(slope, k_off)
        gq_ref[:, cols] = acc * SCALE

    for index in range(4):
        blocks.arrive(do_ref, dwin, ds_, dr, index)
        blocks.arrive(delta_ref, twin, ts, tr, index)

    @pl.loop(0, heads)
    def _(h):
        cols = pl.ds(pl.multiple_of(h * HEAD_DIM, HEAD_DIM), HEAD_DIM)
        kh, vh = k_ref[:, cols], v_ref[:, cols]
        gv, gk = gv_ref[:, cols], gk_ref[:, cols]
        for index in range(4):
            q_off, g_off = qwin[index, :, cols], dwin[index, :, cols]
            prob, slope = pair(q_off, kh, vh, g_off, swin.at[index], twin.at[index], h)
            gv = gv + dot_nn(prob, g_off)
            gk = gk + dot_nn(slope, q_off)
        gv_ref[:, cols] = gv
        gk_ref[:, cols] = gk * SCALE

    firsts[1].wait_recv()
    near_rows = ffn_rows(group.me)
    for ch in range(CHUNKS):
        sl = slice(ch * rows, (ch + 1) * rows)
        seconds[ch].wait_recv()
        enc_ref[sl] = unit_ref[sl] * gain_ref[...] + (
            near_rows[sl].astype(F32) + rbuf1[1, sl].astype(F32) + rbuf2[ch].astype(F32)
        )
    for copy in firsts + seconds:
        copy.wait_send()
    blocks.left(do_ref, dwin, ds_, dr)
    blocks.left(delta_ref, twin, ts, tr)


def pair_off(queries, keys, values, grads, stats, delta_row, h, live):
    heads = stats.shape[0] // 2
    bias = (live - 1.0) * 1e30
    prob = jnp.exp(dot_nt(keys, queries) * SCALE + bias - stats[pl.ds(h, 1), :])
    prob = prob * stats[pl.ds(heads + h, 1), :]
    slope = (prob * (dot_nt(values, grads) - delta_row[pl.ds(h, 1), :])).astype(BF16)
    return None, slope


def grads_stage(count, low, w, att, q, k, v, kwin, vwin, qwin, stats, swin, ffn, unit, gain):
    tok, width = low.shape
    own = unit.shape[0]
    dma = pltpu.SemaphoreType.DMA
    vm = pl.BlockSpec(memory_space=VM)
    chunk = VM((CHUNKS, own // CHUNKS, width), BF16)
    grad = jax.ShapeDtypeStruct(q.shape, F32)
    return pl.pallas_call(
        functools.partial(grads_kernel, count),
        out_shape=(jax.ShapeDtypeStruct((own, width), F32), grad, grad, grad),
        in_specs=[vm] * 14,
        out_specs=(vm,) * 4,
        scratch_shapes=[
            VM((4,) + q.shape, BF16),
            VM((4, 8, tok), F32),
            VM(q.shape, BF16),
            VM((8, tok), F32),
            VM((2, own, width), BF16),
            chunk,
            chunk,
        ]
        + [dma((4,))] * 4
        + reduce_sems(),
        compiler_params=pltpu.CompilerParams(
            collective_id=4, has_side_effects=True, vmem_limit_bytes=48 << 20
        ),
        name="grads_stage",
    )(low, w, att, q, k, v, kwin, vwin, qwin, stats, swin, ffn, unit, gain)


def gelu_slope(inputs):
    output, pull_back = jax.vjp(jax.nn.gelu, inputs)
    return (output, pull_back(jnp.ones_like(inputs))[0])


def shards(
    count,
    groups,
    query_heads,
    key_heads,
    value_heads,
    residual,
    out_weight,
    ln_gain,
    up_source,
    down_source,
    copy_gain,
    neuron_source,
    cotangent,
):
    model_width = residual.shape[1]
    tp_place = lax.axis_index("tp")
    gain = ln_gain[None, :]
    src_width = up_source.shape[1]
    local_source = neuron_source - tp_place * src_width
    pick = (
        lax.broadcasted_iota(jnp.int32, (src_width, local_source.shape[0]), 0)
        == local_source[None, :]
    )
    counts = 1.0 + jnp.sum(pick.astype(F32), axis=1)
    inverse = 1.0 / counts
    pick = pick.astype(BF16)

    attended, kwin, vwin, stats = attend(count, query_heads, key_heads, value_heads)
    normed, unit, sigma, qwin, swin = norm_stage(
        count, groups, attended, out_weight, residual, gain, query_heads, stats
    )
    hidden_in = dot_nn(normed, up_source)
    copies_in = dot_nn(hidden_in.astype(BF16), pick) * copy_gain
    act_src, slope_src = gelu_slope(hidden_in)
    act_copy, slope_copy = gelu_slope(copies_in)
    merged = ((act_src + dot_nt(act_copy.astype(BF16), pick)) * inverse).astype(BF16)
    grad_scaled = dot_nt(cotangent, down_source) * inverse
    grad_copy = dot_nn(grad_scaled.astype(BF16), pick) * slope_copy
    grad_hidden = (
        grad_scaled * slope_src + dot_nt((grad_copy * copy_gain).astype(BF16), pick)
    ).astype(BF16)
    ffn_part = dot_nn(merged, down_source).astype(BF16)
    grad_low = back_stage(groups, grad_hidden, up_source, cotangent, gain, unit, sigma)
    encoded, grad_query, grad_key, grad_value = grads_stage(
        count, grad_low, out_weight, attended, query_heads, key_heads, value_heads,
        kwin, vwin, qwin, stats, swin, ffn_part, unit, gain,
    )
    col_width = model_width // groups
    grad_residual = lax.dynamic_slice_in_dim(grad_low, tp_place * col_width, col_width, 1)
    return (encoded, grad_query, grad_key, grad_value, grad_residual.astype(F32))


def solution(mesh):
    in_specs = (
        P("seq", "tp"),
        P("seq", "tp"),
        P("seq", "tp"),
        P("seq", None),
        P("tp", None),
        P(),
        P(None, "tp"),
        P("tp", None),
        P("tp"),
        P("tp"),
        P("seq", None),
    )
    out_specs = (
        P(("seq", "tp"), None),
        P("seq", "tp"),
        P("seq", "tp"),
        P("seq", "tp"),
        P("seq", "tp"),
    )
    body = functools.partial(shards, mesh.shape["seq"], mesh.shape["tp"])
    return jax.shard_map(body, mesh=mesh, in_specs=in_specs, out_specs=out_specs, check_vma=False)
```

```python
import functools
import math

import jax
import jax.numpy as jnp
from jax import lax
from jax.experimental import pallas as pl
from jax.experimental.pallas import tpu as pltpu
from jax.sharding import PartitionSpec as P

HEAD_DIM = 128
OFFSETS = (-2, -1, 1, 2)
CHUNKS = 4
TILE = 512
epsilon = 1e-05
MESH = pl.DeviceIdType.MESH
VM = pltpu.VMEM
F32 = jnp.float32
BF16 = jnp.bfloat16
SCALE = 1.0 / math.sqrt(HEAD_DIM)


def dot_nn(a, b):
    return jnp.dot(a, b, preferred_element_type=F32)


def dot_nt(a, b):
    return lax.dot_general(a, b, (((1,), (1,)), ((), ())), preferred_element_type=F32)


def dot_tn(a, b):
    return lax.dot_general(a, b, (((0,), (0,)), ((), ())), preferred_element_type=F32)


def remote(src, dst, send, recv, **where):
    return pltpu.make_async_remote_copy(
        src_ref=src, dst_ref=dst, send_sem=send, recv_sem=recv, device_id=where, device_id_type=MESH
    )


class Blocks:
    def __init__(self, count):
        self.count = count
        self.place = lax.axis_index("seq")

    def there(self, offset):
        other = self.place + offset
        return (other >= 0) & (other < self.count)

    def greet(self, barrier):
        for offset in OFFSETS:
            @pl.when(self.there(offset))
            def _():
                pl.semaphore_signal(
                    barrier, inc=1, device_id={"seq": self.place + offset}, device_id_type=MESH
                )

    def greeted(self, barrier, more=0):
        peers = sum(self.there(offset).astype(jnp.int32) for offset in OFFSETS)
        pl.semaphore_wait(barrier, peers + more)

    def copy(self, src, window, send, recv, to, slot, sent):
        return remote(src, window.at[slot], send.at[sent], recv.at[slot], seq=self.place + to)

    def send(self, src, window, send, recv):
        for index, offset in enumerate(OFFSETS):
            @pl.when(self.there(offset))
            def _():
                self.copy(src, window, send, recv, offset, 3 - index, index).start()

    def clear(self, window):
        for index, offset in enumerate(OFFSETS):
            @pl.when(jnp.logical_not(self.there(offset)))
            def _():
                window[index] = jnp.zeros(window.shape[1:], window.dtype)

    def arrive(self, src, window, send, recv, index):
        offset = OFFSETS[index]
        @pl.when(self.there(offset))
        def _():
            self.copy(src, window, send, recv, offset, index, index).wait_recv()

    def left(self, src, window, send, recv):
        for index, offset in enumerate(OFFSETS):
            @pl.when(self.there(offset))
            def _():
                self.copy(src, window, send, recv, offset, 3 - index, index).wait_send()


class Group:
    def __init__(self):
        me = lax.axis_index("tp")
        chip, core = lax.div(me, 2), lax.rem(me, 2)
        self.me = me
        self.sibling = chip * 2 + 1 - core
        self.far = (1 - chip) * 2 + core
        self.across = (1 - chip) * 2 + 1 - core

    def greet(self, barrier):
        for other in (self.sibling, self.far):
            pl.semaphore_signal(barrier, inc=1, device_id={"tp": other}, device_id_type=MESH)


def attend_kernel(
    count, q_ref, k_ref, v_ref, cot_ref, down_ref,
    out_ref, kwin, vwin, stat_ref, gm_ref,
    prob, cot_buf, down_buf, ks, kr, vs, vr, cot_sem, down_sem,
):
    blocks = Blocks(count)
    pieces, depth = down_buf.shape[:2]
    cot_copy = pltpu.make_async_copy(cot_ref, cot_buf, cot_sem)
    cot_copy.start()
    loads = [
        pltpu.make_async_copy(
            down_ref.at[pl.ds(i * depth, depth)], down_buf.at[i], down_sem.at[i]
        )
        for i in range(pieces)
    ]
    for load in loads:
        load.start()
    barrier = pltpu.get_barrier_semaphore()
    blocks.greet(barrier)
    blocks.greeted(barrier)
    blocks.send(k_ref, kwin, ks, kr)
    blocks.send(v_ref, vwin, vs, vr)
    blocks.clear(kwin)
    blocks.clear(vwin)
    rows, width = q_ref.shape
    heads = width // HEAD_DIM
    cot_copy.wait()
    for i in range(pieces):
        loads[i].wait()
        gm_ref[:, i * depth : (i + 1) * depth] = dot_nt(cot_buf[...], down_buf[i])
    for index in range(4):
        blocks.arrive(k_ref, kwin, ks, kr, index)
    bias = [jnp.where(blocks.there(offset), 0.0, -1e30).astype(F32) for offset in OFFSETS]
    lane = lax.broadcasted_iota(jnp.int32, (rows, 128), 1)
    stats = jnp.zeros((rows, 128), F32)
    for h in range(heads):
        cols = slice(h * HEAD_DIM, (h + 1) * HEAD_DIM)
        qh = q_ref[:, cols]
        scores = [dot_nt(qh, k_ref[:, cols]) * SCALE]
        for index in range(4):
            scores.append(dot_nt(qh, kwin[index, :, cols]) * SCALE + bias[index])
        top = scores[0]
        for s in scores[1:]:
            top = jnp.maximum(top, s)
        top = jnp.max(top, axis=1, keepdims=True)
        exps = [jnp.exp(s - top) for s in scores]
        total = exps[0]
        for e in exps[1:]:
            total = total + e
        inverse = 1.0 / jnp.sum(total, axis=1, keepdims=True)
        for index in range(5):
            prob[h, index] = (exps[index] * inverse).astype(BF16)
        stats = jnp.where(lane == h, top, stats)
        stats = jnp.where(lane == heads + h, inverse, stats)
    stat_ref[...] = jnp.transpose(stats)[: 2 * heads]
    for index in range(4):
        blocks.arrive(v_ref, vwin, vs, vr, index)
    for h in range(heads):
        cols = slice(h * HEAD_DIM, (h + 1) * HEAD_DIM)
        acc = dot_nn(prob[h, 0], v_ref[:, cols])
        for index in range(4):
            acc = acc + dot_nn(prob[h, index + 1], vwin[index, :, cols])
        out_ref[:, cols] = acc.astype(BF16)
    blocks.left(k_ref, kwin, ks, kr)
    blocks.left(v_ref, vwin, vs, vr)


def attend(count, q, k, v, cotangent, down):
    rows, width = q.shape
    src, model = down.shape
    pieces = 4
    heads = width // HEAD_DIM
    win = jax.ShapeDtypeStruct((4, rows, width), BF16)
    dma = pltpu.SemaphoreType.DMA((4,))
    return pl.pallas_call(
        functools.partial(attend_kernel, count),
        out_shape=(
            jax.ShapeDtypeStruct((rows, width), BF16),
            win,
            win,
            jax.ShapeDtypeStruct((2 * heads, rows), F32),
            jax.ShapeDtypeStruct((rows, src), F32),
        ),
        in_specs=[pl.BlockSpec(memory_space=VM)] * 3 + [pl.BlockSpec(memory_space=pl.ANY)] * 2,
        out_specs=(pl.BlockSpec(memory_space=VM),) * 5,
        scratch_shapes=[
            VM((heads, 5, rows, rows), BF16),
            VM(cotangent.shape, BF16),
            VM((pieces, src // pieces, model), BF16),
            dma, dma, dma, dma,
            pltpu.SemaphoreType.DMA(()),
            pltpu.SemaphoreType.DMA((pieces,)),
        ],
        compiler_params=pltpu.CompilerParams(
            collective_id=1, has_side_effects=True, vmem_limit_bytes=48 << 20
        ),
        name="attend",
    )(q, k, v, cotangent, down)


def reduce_first(group, own, part, mine, sbuf1, rbuf1, s1, r1):
    part((group.across, group.sibling), sbuf1)
    copies = [
        remote(sbuf1.at[i], rbuf1.at[i], s1.at[i], r1.at[i], tp=group.sibling) for i in range(2)
    ]
    for copy in copies:
        copy.start()
    part((group.far, group.me), mine)
    return copies


def reduce_second(group, own, mine, rbuf1, sbuf2, rbuf2, s2, r2, copies):
    copies[0].wait_recv()
    rows = own // CHUNKS
    out = []
    for ch in range(CHUNKS):
        sl = slice(ch * rows, (ch + 1) * rows)
        sbuf2[ch] = (mine[0, sl].astype(F32) + rbuf1[0, sl].astype(F32)).astype(BF16)
        copy = remote(sbuf2.at[ch], rbuf2.at[ch], s2.at[ch], r2.at[ch], tp=group.far)
        copy.start()
        out.append(copy)
    copies[1].wait_recv()
    return out


def spread(group, own, full, finish, seconds, ags, agr):
    rows = own // CHUNKS

    def at(owner, ch):
        return full.at[pl.ds(pl.multiple_of(owner * own + ch * rows, rows), rows)]

    to_sib, to_far, passed = [], [], []
    for ch in range(CHUNKS):
        seconds[ch].wait_recv()
        finish(ch, at(group.me, ch))
        mine = at(group.me, ch)
        to_far.append(remote(mine, mine, ags.at[ch, 0], agr.at[ch, 0], tp=group.far))
        to_far[ch].start()
        to_sib.append(remote(mine, mine, ags.at[ch, 1], agr.at[ch, 1], tp=group.sibling))
        to_sib[ch].start()
    for ch in range(CHUNKS):
        to_far[ch].wait_recv()
        got = at(group.far, ch)
        passed.append(remote(got, got, ags.at[ch, 2], agr.at[ch, 2], tp=group.sibling))
        passed[ch].start()
    for ch in range(CHUNKS):
        to_sib[ch].wait_recv()
        passed[ch].wait_recv()
    return to_sib + to_far + passed


def norm_kernel(
    count, att_ref, w_ref, res_ref, gain_ref, q_ref, stat_ref,
    full, unit_ref, sigma_ref, qwin, swin,
    mine, sbuf1, rbuf1, sbuf2, rbuf2, res_buf,
    s1, r1, s2, r2, ags, agr, qs, qr, ss, sr, res_sem,
):
    blocks, group = Blocks(count), Group()
    own, width = unit_ref.shape
    rows = own // CHUNKS
    fetch = pltpu.make_async_copy(
        res_ref.at[pl.ds(pl.multiple_of(group.me * own, own), own)], res_buf, res_sem
    )
    fetch.start()
    barrier = pltpu.get_barrier_semaphore()
    group.greet(barrier)
    blocks.greet(barrier)
    blocks.greeted(barrier, 2)
    blocks.send(q_ref, qwin, qs, qr)
    blocks.send(stat_ref, swin, ss, sr)

    def part(owners, dst):
        lhs = jnp.concatenate(
            [att_ref[pl.ds(pl.multiple_of(o * own, own), own), :] for o in owners], axis=0
        )

        @pl.loop(0, width // TILE)
        def _(ct):
            cols = pl.ds(pl.multiple_of(ct * TILE, TILE), TILE)
            r = dot_nn(lhs, w_ref[:, cols]).astype(BF16)
            dst[0, :, cols] = r[:own]
            dst[1, :, cols] = r[own:]

    firsts = reduce_first(group, own, part, mine, sbuf1, rbuf1, s1, r1)
    blocks.clear(qwin)
    blocks.clear(swin)
    seconds = reduce_second(group, own, mine, rbuf1, sbuf2, rbuf2, s2, r2, firsts)
    fetch.wait()

    def finish(ch, dst):
        sl = slice(ch * rows, (ch + 1) * rows)
        stream = (
            res_buf[sl].astype(F32)
            + mine[1, sl].astype(F32)
            + rbuf1[1, sl].astype(F32)
            + rbuf2[ch].astype(F32)
        )
        centered = stream - jnp.mean(stream, axis=1, keepdims=True)
        sigma = jnp.sqrt(jnp.mean(centered * centered, axis=1, keepdims=True) + epsilon)
        unit = centered / sigma
        unit_ref[sl] = unit
        sigma_ref[sl] = jnp.broadcast_to(sigma, (rows, 128))
        dst[...] = (unit * gain_ref[...]).astype(BF16)

    tails = spread(group, own, full, finish, seconds, ags, agr)
    for copy in firsts + seconds + tails:
        copy.wait_send()
    for index in range(4):
        blocks.arrive(q_ref, qwin, qs, qr, index)
        blocks.arrive(stat_ref, swin, ss, sr, index)
    blocks.left(q_ref, qwin, qs, qr)
    blocks.left(stat_ref, swin, ss, sr)


def reduce_scratch(own, width):
    two = VM((2, own, width), BF16)
    chunk = VM((CHUNKS, own // CHUNKS, width), BF16)
    return [two, two, two, chunk, chunk]


def reduce_sems():
    dma = pltpu.SemaphoreType.DMA
    return [dma((2,)), dma((2,)), dma((CHUNKS,)), dma((CHUNKS,))]


def norm_stage(count, groups, att, w, residual, gain, q, stats):
    tok, width = residual.shape
    own = tok // groups
    dma = pltpu.SemaphoreType.DMA
    vm = pl.BlockSpec(memory_space=VM)
    return pl.pallas_call(
        functools.partial(norm_kernel, count),
        out_shape=(
            jax.ShapeDtypeStruct((tok, width), BF16),
            jax.ShapeDtypeStruct((own, width), F32),
            jax.ShapeDtypeStruct((own, 128), F32),
            jax.ShapeDtypeStruct((4,) + q.shape, BF16),
            jax.ShapeDtypeStruct((4,) + stats.shape, F32),
        ),
        in_specs=[vm, vm, pl.BlockSpec(memory_space=pl.ANY), vm, vm, vm],
        out_specs=(vm,) * 5,
        scratch_shapes=reduce_scratch(own, width)
        + [VM((own, width), BF16)]
        + reduce_sems()
        + [dma((CHUNKS, 3)), dma((CHUNKS, 3))]
        + [dma((4,))] * 4
        + [dma(())],
        compiler_params=pltpu.CompilerParams(
            collective_id=2, has_side_effects=True, vmem_limit_bytes=40 << 20
        ),
        name="norm_stage",
    )(att, w, residual, gain, q, stats)


def back_kernel(
    gh_ref, up_ref, merged_ref, down_ref, cot_ref, gain_ref, unit_ref, sigma_ref,
    full, ffn_ref,
    mine, sbuf1, rbuf1, sbuf2, rbuf2, cot_buf, w_ref, down_buf,
    s1, r1, s2, r2, ags, agr, cot_sem, up_sem, down_sem,
):
    group = Group()
    own, width = unit_ref.shape
    rows = own // CHUNKS
    tiles = width // TILE

    def up_load(ct):
        span = pl.ds(pl.multiple_of(ct * TILE, TILE), TILE)
        return pltpu.make_async_copy(up_ref.at[span], w_ref.at[span], up_sem.at[ct])

    def down_load(ct):
        span = pl.ds(pl.multiple_of(ct * TILE, TILE), TILE)
        return pltpu.make_async_copy(down_ref.at[:, span], down_buf.at[ct], down_sem.at[ct])

    for ct in range(tiles):
        up_load(ct).start()
    fetch = pltpu.make_async_copy(
        cot_ref.at[pl.ds(pl.multiple_of(group.me * own, own), own)], cot_buf, cot_sem
    )
    fetch.start()
    barrier = pltpu.get_barrier_semaphore()
    group.greet(barrier)
    pl.semaphore_wait(barrier, 2)

    def part(owners, dst):
        lhs = jnp.concatenate(
            [gh_ref[pl.ds(pl.multiple_of(o * own, own), own), :] for o in owners], axis=0
        )

        @pl.loop(0, tiles)
        def _(ct):
            if dst is sbuf1:
                up_load(ct).wait()
            cols = pl.ds(pl.multiple_of(ct * TILE, TILE), TILE)
            r = dot_nt(lhs, w_ref[cols, :]).astype(BF16)
            dst[0, :, cols] = r[:own]
            dst[1, :, cols] = r[own:]

    for ct in range(tiles):
        down_load(ct).start()
    firsts = reduce_first(group, own, part, mine, sbuf1, rbuf1, s1, r1)
    seconds = reduce_second(group, own, mine, rbuf1, sbuf2, rbuf2, s2, r2, firsts)
    fetch.wait()

    @pl.loop(0, tiles)
    def _(ct):
        down_load(ct).wait()
        cols = pl.ds(pl.multiple_of(ct * TILE, TILE), TILE)
        ffn_ref[:, cols] = dot_nn(merged_ref[...], down_buf[ct]).astype(BF16)

    def finish(ch, dst):
        sl = slice(ch * rows, (ch + 1) * rows)
        grad = (
            cot_buf[sl].astype(F32)
            + mine[1, sl].astype(F32)
            + rbuf1[1, sl].astype(F32)
            + rbuf2[ch].astype(F32)
        )
        scaled = grad * gain_ref[...]
        unit = unit_ref[sl]
        mean = jnp.mean(scaled, axis=1, keepdims=True)
        along = jnp.mean(scaled * unit, axis=1, keepdims=True)
        dst[...] = ((scaled - mean - unit * along) / sigma_ref[sl, :1]).astype(BF16)

    tails = spread(group, own, full, finish, seconds, ags, agr)
    for copy in firsts + seconds + tails:
        copy.wait_send()


def back_stage(groups, gh, up, merged, down, cotangent, gain, unit, sigma):
    tok, width = cotangent.shape
    own = tok // groups
    dma = pltpu.SemaphoreType.DMA
    vm = pl.BlockSpec(memory_space=VM)
    far = pl.BlockSpec(memory_space=pl.ANY)
    tiles = width // TILE
    return pl.pallas_call(
        back_kernel,
        out_shape=(jax.ShapeDtypeStruct((tok, width), BF16),) * 2,
        in_specs=[vm, far, vm, far, far, vm, vm, vm],
        out_specs=(vm, vm),
        scratch_shapes=reduce_scratch(own, width)
        + [VM((own, width), BF16), VM(up.shape, BF16), VM((tiles, down.shape[0], TILE), BF16)]
        + reduce_sems()
        + [dma((CHUNKS, 3)), dma((CHUNKS, 3)), dma(()), dma((tiles,)), dma((tiles,))],
        compiler_params=pltpu.CompilerParams(
            collective_id=3, has_side_effects=True, vmem_limit_bytes=48 << 20
        ),
        name="back_stage",
    )(gh, up, merged, down, cotangent, gain, unit, sigma)


def grads_kernel(
    count, low_ref, w_ref, att_ref, q_ref, k_ref, v_ref, kwin, vwin, qwin, stat_ref, swin,
    ffn_ref, unit_ref, gain_ref,
    enc_ref, gq_ref, gk_ref, gv_ref,
    dwin, twin, do_ref, delta_ref, rbuf1, sbuf2, rbuf2,
    ds_, dr, ts, tr, s1, r1, s2, r2,
):
    blocks, group = Blocks(count), Group()
    own, width = unit_ref.shape
    tok, cols_all = q_ref.shape
    heads = cols_all // HEAD_DIM
    rows = own // CHUNKS
    barrier = pltpu.get_barrier_semaphore()
    group.greet(barrier)
    blocks.greet(barrier)
    blocks.greeted(barrier, 2)

    def ffn_rows(owner):
        return ffn_ref.at[pl.ds(pl.multiple_of(owner * own, own), own)]

    firsts = [
        remote(ffn_rows(owner), rbuf1.at[i], s1.at[i], r1.at[i], tp=group.sibling)
        for i, owner in enumerate((group.across, group.sibling))
    ]
    for copy in firsts:
        copy.start()
    lane = lax.broadcasted_iota(jnp.int32, (tok, 128), 1)
    grad_att = dot_nt(low_ref[...], w_ref[...]).astype(BF16)
    do_ref[...] = grad_att
    blocks.send(do_ref, dwin, ds_, dr)
    deltas = jnp.zeros((tok, 128), F32)
    for h in range(heads):
        cols = slice(h * HEAD_DIM, (h + 1) * HEAD_DIM)
        delta = jnp.sum(
            grad_att[:, cols].astype(F32) * att_ref[:, cols].astype(F32), axis=1, keepdims=True
        )
        deltas = jnp.where(lane == h, delta, deltas)
    delta_ref[...] = jnp.transpose(deltas)[:8]
    blocks.send(delta_ref, twin, ts, tr)
    blocks.clear(dwin)
    blocks.clear(twin)
    firsts[0].wait_recv()
    seconds = []
    far_rows = ffn_rows(group.far)
    for ch in range(CHUNKS):
        sl = slice(ch * rows, (ch + 1) * rows)
        sbuf2[ch] = (far_rows[sl].astype(F32) + rbuf1[0, sl].astype(F32)).astype(BF16)
        seconds.append(remote(sbuf2.at[ch], rbuf2.at[ch], s2.at[ch], r2.at[ch], tp=group.far))
        seconds[ch].start()

    def pair(queries, keys, values, grads, stats, delta_row, h):
        top = stats[pl.ds(h, 1), :]
        inverse = stats[pl.ds(heads + h, 1), :]
        prob = jnp.exp(dot_nt(keys, queries) * SCALE - top) * inverse
        slope = (prob * (dot_nt(values, grads) - delta_row[pl.ds(h, 1), :])).astype(BF16)
        return prob.astype(BF16), slope

    @pl.loop(0, heads)
    def _(h):
        cols = pl.ds(pl.multiple_of(h * HEAD_DIM, HEAD_DIM), HEAD_DIM)
        qh, gh = q_ref[:, cols], do_ref[:, cols]
        kh, vh = k_ref[:, cols], v_ref[:, cols]
        prob, slope = pair(qh, kh, vh, gh, stat_ref, delta_ref, h)
        gv_ref[:, cols] = dot_nn(prob, gh)
        gk_ref[:, cols] = dot_nn(slope, qh)
        acc = dot_tn(slope, kh)
        for index in range(4):
            k_off, v_off = kwin[index, :, cols], vwin[index, :, cols]
            live = jnp.where(blocks.there(OFFSETS[index]), 1.0, 0.0).astype(F32)
            _, slope = pair_off(qh, k_off, v_off, gh, stat_ref, delta_ref, h, live)
            acc = acc + dot_tn(slope, k_off)
        gq_ref[:, cols] = acc * SCALE

    for index in range(4):
        blocks.arrive(do_ref, dwin, ds_, dr, index)
        blocks.arrive(delta_ref, twin, ts, tr, index)

        @pl.when(blocks.there(OFFSETS[index]))
        def _():
            @pl.loop(0, heads)
            def _(h):
                cols = pl.ds(pl.multiple_of(h * HEAD_DIM, HEAD_DIM), HEAD_DIM)
                kh, vh = k_ref[:, cols], v_ref[:, cols]
                q_off, g_off = qwin[index, :, cols], dwin[index, :, cols]
                prob, slope = pair(q_off, kh, vh, g_off, swin.at[index], twin.at[index], h)
                gv_ref[:, cols] += dot_nn(prob, g_off)
                gk_ref[:, cols] += dot_nn(slope, q_off)

    gk_ref[...] = gk_ref[...] * SCALE

    firsts[1].wait_recv()
    near_rows = ffn_rows(group.me)
    for ch in range(CHUNKS):
        sl = slice(ch * rows, (ch + 1) * rows)
        seconds[ch].wait_recv()
        enc_ref[sl] = unit_ref[sl] * gain_ref[...] + (
            near_rows[sl].astype(F32) + rbuf1[1, sl].astype(F32) + rbuf2[ch].astype(F32)
        )
    for copy in firsts + seconds:
        copy.wait_send()
    blocks.left(do_ref, dwin, ds_, dr)
    blocks.left(delta_ref, twin, ts, tr)


def pair_off(queries, keys, values, grads, stats, delta_row, h, live):
    heads = stats.shape[0] // 2
    bias = (live - 1.0) * 1e30
    prob = jnp.exp(dot_nt(keys, queries) * SCALE + bias - stats[pl.ds(h, 1), :])
    prob = prob * stats[pl.ds(heads + h, 1), :]
    slope = (prob * (dot_nt(values, grads) - delta_row[pl.ds(h, 1), :])).astype(BF16)
    return None, slope


def grads_stage(count, low, w, att, q, k, v, kwin, vwin, qwin, stats, swin, ffn, unit, gain):
    tok, width = low.shape
    own = unit.shape[0]
    dma = pltpu.SemaphoreType.DMA
    vm = pl.BlockSpec(memory_space=VM)
    chunk = VM((CHUNKS, own // CHUNKS, width), BF16)
    grad = jax.ShapeDtypeStruct(q.shape, F32)
    return pl.pallas_call(
        functools.partial(grads_kernel, count),
        out_shape=(jax.ShapeDtypeStruct((own, width), F32), grad, grad, grad),
        in_specs=[vm] * 14,
        out_specs=(vm,) * 4,
        scratch_shapes=[
            VM((4,) + q.shape, BF16),
            VM((4, 8, tok), F32),
            VM(q.shape, BF16),
            VM((8, tok), F32),
            VM((2, own, width), BF16),
            chunk,
            chunk,
        ]
        + [dma((4,))] * 4
        + reduce_sems(),
        compiler_params=pltpu.CompilerParams(
            collective_id=4, has_side_effects=True, vmem_limit_bytes=48 << 20
        ),
        name="grads_stage",
    )(low, w, att, q, k, v, kwin, vwin, qwin, stats, swin, ffn, unit, gain)


def gelu_slope(inputs):
    output, pull_back = jax.vjp(jax.nn.gelu, inputs)
    return (output, pull_back(jnp.ones_like(inputs))[0])


def shards(
    count,
    groups,
    query_heads,
    key_heads,
    value_heads,
    residual,
    out_weight,
    ln_gain,
    up_source,
    down_source,
    copy_gain,
    neuron_source,
    cotangent,
):
    model_width = residual.shape[1]
    tp_place = lax.axis_index("tp")
    gain = ln_gain[None, :]
    src_width = up_source.shape[1]
    local_source = neuron_source - tp_place * src_width
    pick = (
        lax.broadcasted_iota(jnp.int32, (src_width, local_source.shape[0]), 0)
        == local_source[None, :]
    )
    counts = 1.0 + jnp.sum(pick.astype(F32), axis=1)
    inverse = 1.0 / counts
    pick = pick.astype(BF16)

    attended, kwin, vwin, stats, grad_merged = attend(
        count, query_heads, key_heads, value_heads, cotangent, down_source
    )
    normed, unit, sigma, qwin, swin = norm_stage(
        count, groups, attended, out_weight, residual, gain, query_heads, stats
    )
    hidden_in = dot_nn(normed, up_source)
    copies_in = dot_nn(hidden_in.astype(BF16), pick) * copy_gain
    act_src, slope_src = gelu_slope(hidden_in)
    act_copy, slope_copy = gelu_slope(copies_in)
    merged = ((act_src + dot_nt(act_copy.astype(BF16), pick)) * inverse).astype(BF16)
    grad_scaled = grad_merged * inverse
    grad_copy = dot_nn(grad_scaled.astype(BF16), pick) * slope_copy
    grad_hidden = (
        grad_scaled * slope_src + dot_nt((grad_copy * copy_gain).astype(BF16), pick)
    ).astype(BF16)
    grad_low, ffn_part = back_stage(
        groups, grad_hidden, up_source, merged, down_source, cotangent, gain, unit, sigma
    )
    encoded, grad_query, grad_key, grad_value = grads_stage(
        count, grad_low, out_weight, attended, query_heads, key_heads, value_heads,
        kwin, vwin, qwin, stats, swin, ffn_part, unit, gain,
    )
    col_width = model_width // groups
    grad_residual = lax.dynamic_slice_in_dim(grad_low, tp_place * col_width, col_width, 1)
    return (encoded, grad_query, grad_key, grad_value, grad_residual.astype(F32))


def solution(mesh):
    in_specs = (
        P("seq", "tp"),
        P("seq", "tp"),
        P("seq", "tp"),
        P("seq", None),
        P("tp", None),
        P(),
        P(None, "tp"),
        P("tp", None),
        P("tp"),
        P("tp"),
        P("seq", None),
    )
    out_specs = (
        P(("seq", "tp"), None),
        P("seq", "tp"),
        P("seq", "tp"),
        P("seq", "tp"),
        P("seq", "tp"),
    )
    body = functools.partial(shards, mesh.shape["seq"], mesh.shape["tp"])
    return jax.shard_map(body, mesh=mesh, in_specs=in_specs, out_specs=out_specs, check_vma=False)
```

```python
import functools
import math

import jax
import jax.numpy as jnp
from jax import lax
from jax.experimental import pallas as pl
from jax.experimental.pallas import tpu as pltpu
from jax.sharding import PartitionSpec as P

HEAD_DIM = 128
OFFSETS = (-2, -1, 1, 2)
CHUNKS = 4
TILE = 512
epsilon = 1e-05
MESH = pl.DeviceIdType.MESH
VM = pltpu.VMEM
F32 = jnp.float32
BF16 = jnp.bfloat16
SCALE = 1.0 / math.sqrt(HEAD_DIM)


def dot_nn(a, b):
    return jnp.dot(a, b, preferred_element_type=F32)


def dot_nt(a, b):
    return lax.dot_general(a, b, (((1,), (1,)), ((), ())), preferred_element_type=F32)


def dot_tn(a, b):
    return lax.dot_general(a, b, (((0,), (0,)), ((), ())), preferred_element_type=F32)


def remote(src, dst, send, recv, **where):
    return pltpu.make_async_remote_copy(
        src_ref=src, dst_ref=dst, send_sem=send, recv_sem=recv, device_id=where, device_id_type=MESH
    )


class Blocks:
    def __init__(self, count):
        self.count = count
        self.place = lax.axis_index("seq")

    def there(self, offset):
        other = self.place + offset
        return (other >= 0) & (other < self.count)

    def greet(self, barrier):
        for offset in OFFSETS:
            @pl.when(self.there(offset))
            def _():
                pl.semaphore_signal(
                    barrier, inc=1, device_id={"seq": self.place + offset}, device_id_type=MESH
                )

    def greeted(self, barrier, more=0):
        peers = sum(self.there(offset).astype(jnp.int32) for offset in OFFSETS)
        pl.semaphore_wait(barrier, peers + more)

    def copy(self, src, window, send, recv, to, slot, sent):
        return remote(src, window.at[slot], send.at[sent], recv.at[slot], seq=self.place + to)

    def send(self, src, window, send, recv):
        for index, offset in enumerate(OFFSETS):
            @pl.when(self.there(offset))
            def _():
                self.copy(src, window, send, recv, offset, 3 - index, index).start()

    def clear(self, window):
        for index, offset in enumerate(OFFSETS):
            @pl.when(jnp.logical_not(self.there(offset)))
            def _():
                window[index] = jnp.zeros(window.shape[1:], window.dtype)

    def arrive(self, src, window, send, recv, index):
        offset = OFFSETS[index]
        @pl.when(self.there(offset))
        def _():
            self.copy(src, window, send, recv, offset, index, index).wait_recv()

    def left(self, src, window, send, recv):
        for index, offset in enumerate(OFFSETS):
            @pl.when(self.there(offset))
            def _():
                self.copy(src, window, send, recv, offset, 3 - index, index).wait_send()


class Group:
    def __init__(self):
        me = lax.axis_index("tp")
        chip, core = lax.div(me, 2), lax.rem(me, 2)
        self.me = me
        self.sibling = chip * 2 + 1 - core
        self.far = (1 - chip) * 2 + core
        self.across = (1 - chip) * 2 + 1 - core

    def greet(self, barrier):
        for other in (self.sibling, self.far):
            pl.semaphore_signal(barrier, inc=1, device_id={"tp": other}, device_id_type=MESH)


def attend_kernel(
    count, q_ref, k_ref, v_ref, cot_ref, down_ref,
    out_ref, kwin, vwin, stat_ref, gm_ref,
    prob, cot_buf, down_buf, ks, kr, vs, vr, cot_sem, down_sem,
):
    blocks = Blocks(count)
    pieces, depth = down_buf.shape[:2]
    cot_copy = pltpu.make_async_copy(cot_ref, cot_buf, cot_sem)
    cot_copy.start()
    loads = [
        pltpu.make_async_copy(
            down_ref.at[pl.ds(i * depth, depth)], down_buf.at[i], down_sem.at[i]
        )
        for i in range(pieces)
    ]
    for load in loads:
        load.start()
    barrier = pltpu.get_barrier_semaphore()
    blocks.greet(barrier)
    blocks.greeted(barrier)
    blocks.send(k_ref, kwin, ks, kr)
    blocks.send(v_ref, vwin, vs, vr)
    blocks.clear(kwin)
    blocks.clear(vwin)
    rows, width = q_ref.shape
    heads = width // HEAD_DIM
    cot_copy.wait()
    for i in range(pieces):
        loads[i].wait()
        gm_ref[:, i * depth : (i + 1) * depth] = dot_nt(cot_buf[...], down_buf[i])
    for index in range(4):
        blocks.arrive(k_ref, kwin, ks, kr, index)
    bias = [jnp.where(blocks.there(offset), 0.0, -1e30).astype(F32) for offset in OFFSETS]
    lane = lax.broadcasted_iota(jnp.int32, (rows, 128), 1)
    stats = jnp.zeros((rows, 128), F32)
    for h in range(heads):
        cols = slice(h * HEAD_DIM, (h + 1) * HEAD_DIM)
        qh = q_ref[:, cols]
        scores = [dot_nt(qh, k_ref[:, cols]) * SCALE]
        for index in range(4):
            scores.append(dot_nt(qh, kwin[index, :, cols]) * SCALE + bias[index])
        top = scores[0]
        for s in scores[1:]:
            top = jnp.maximum(top, s)
        top = jnp.max(top, axis=1, keepdims=True)
        exps = [jnp.exp(s - top) for s in scores]
        total = exps[0]
        for e in exps[1:]:
            total = total + e
        inverse = 1.0 / jnp.sum(total, axis=1, keepdims=True)
        for index in range(5):
            prob[h, index] = (exps[index] * inverse).astype(BF16)
        stats = jnp.where(lane == h, top, stats)
        stats = jnp.where(lane == heads + h, inverse, stats)
    stat_ref[...] = jnp.transpose(stats)[: 2 * heads]
    for index in range(4):
        blocks.arrive(v_ref, vwin, vs, vr, index)
    for h in range(heads):
        cols = slice(h * HEAD_DIM, (h + 1) * HEAD_DIM)
        acc = dot_nn(prob[h, 0], v_ref[:, cols])
        for index in range(4):
            acc = acc + dot_nn(prob[h, index + 1], vwin[index, :, cols])
        out_ref[:, cols] = acc.astype(BF16)
    blocks.left(k_ref, kwin, ks, kr)
    blocks.left(v_ref, vwin, vs, vr)


def attend(count, q, k, v, cotangent, down):
    rows, width = q.shape
    src, model = down.shape
    pieces = 4
    heads = width // HEAD_DIM
    win = jax.ShapeDtypeStruct((4, rows, width), BF16)
    dma = pltpu.SemaphoreType.DMA((4,))
    return pl.pallas_call(
        functools.partial(attend_kernel, count),
        out_shape=(
            jax.ShapeDtypeStruct((rows, width), BF16),
            win,
            win,
            jax.ShapeDtypeStruct((2 * heads, rows), F32),
            jax.ShapeDtypeStruct((rows, src), F32),
        ),
        in_specs=[pl.BlockSpec(memory_space=VM)] * 3 + [pl.BlockSpec(memory_space=pl.ANY)] * 2,
        out_specs=(pl.BlockSpec(memory_space=VM),) * 5,
        scratch_shapes=[
            VM((heads, 5, rows, rows), BF16),
            VM(cotangent.shape, BF16),
            VM((pieces, src // pieces, model), BF16),
            dma, dma, dma, dma,
            pltpu.SemaphoreType.DMA(()),
            pltpu.SemaphoreType.DMA((pieces,)),
        ],
        compiler_params=pltpu.CompilerParams(
            collective_id=1, has_side_effects=True, vmem_limit_bytes=48 << 20
        ),
        name="attend",
    )(q, k, v, cotangent, down)


def reduce_first(group, own, part, mine, sbuf1, rbuf1, s1, r1):
    part((group.across, group.sibling), sbuf1)
    copies = [
        remote(sbuf1.at[i], rbuf1.at[i], s1.at[i], r1.at[i], tp=group.sibling) for i in range(2)
    ]
    for copy in copies:
        copy.start()
    part((group.far, group.me), mine)
    return copies


def reduce_second(group, own, mine, rbuf1, sbuf2, rbuf2, s2, r2, copies):
    copies[0].wait_recv()
    rows = own // CHUNKS
    out = []
    for ch in range(CHUNKS):
        sl = slice(ch * rows, (ch + 1) * rows)
        sbuf2[ch] = (mine[0, sl].astype(F32) + rbuf1[0, sl].astype(F32)).astype(BF16)
        copy = remote(sbuf2.at[ch], rbuf2.at[ch], s2.at[ch], r2.at[ch], tp=group.far)
        copy.start()
        out.append(copy)
    copies[1].wait_recv()
    return out


def spread(group, own, full, finish, seconds, ags, agr):
    rows = own // CHUNKS

    def at(owner, ch):
        return full.at[pl.ds(pl.multiple_of(owner * own + ch * rows, rows), rows)]

    to_sib, to_far, passed = [], [], []
    for ch in range(CHUNKS):
        seconds[ch].wait_recv()
        finish(ch, at(group.me, ch))
        mine = at(group.me, ch)
        to_far.append(remote(mine, mine, ags.at[ch, 0], agr.at[ch, 0], tp=group.far))
        to_far[ch].start()
        to_sib.append(remote(mine, mine, ags.at[ch, 1], agr.at[ch, 1], tp=group.sibling))
        to_sib[ch].start()
    for ch in range(CHUNKS):
        to_far[ch].wait_recv()
        got = at(group.far, ch)
        passed.append(remote(got, got, ags.at[ch, 2], agr.at[ch, 2], tp=group.sibling))
        passed[ch].start()
    for ch in range(CHUNKS):
        to_sib[ch].wait_recv()
        passed[ch].wait_recv()
    return to_sib + to_far + passed


def norm_kernel(
    count, att_ref, w_ref, res_ref, gain_ref, q_ref, stat_ref,
    up_ref, pick_ref, gm_ref, inv_ref, cg_ref,
    merged_ref, gh_ref, unit_ref, sigma_ref, qwin, swin,
    mine, sbuf1, rbuf1, sbuf2, rbuf2, res_buf, full, up_buf,
    s1, r1, s2, r2, ags, agr, qs, qr, ss, sr, res_sem, up_sem,
):
    blocks, group = Blocks(count), Group()
    own, width = unit_ref.shape
    rows = own // CHUNKS
    fetch = pltpu.make_async_copy(
        res_ref.at[pl.ds(pl.multiple_of(group.me * own, own), own)], res_buf, res_sem
    )
    fetch.start()
    up_load = pltpu.make_async_copy(up_ref, up_buf, up_sem)
    up_load.start()
    barrier = pltpu.get_barrier_semaphore()
    group.greet(barrier)
    blocks.greet(barrier)
    blocks.greeted(barrier, 2)
    blocks.send(q_ref, qwin, qs, qr)
    blocks.send(stat_ref, swin, ss, sr)

    def part(owners, dst):
        lhs = jnp.concatenate(
            [att_ref[pl.ds(pl.multiple_of(o * own, own), own), :] for o in owners], axis=0
        )

        @pl.loop(0, width // TILE)
        def _(ct):
            cols = pl.ds(pl.multiple_of(ct * TILE, TILE), TILE)
            r = dot_nn(lhs, w_ref[:, cols]).astype(BF16)
            dst[0, :, cols] = r[:own]
            dst[1, :, cols] = r[own:]

    firsts = reduce_first(group, own, part, mine, sbuf1, rbuf1, s1, r1)
    blocks.clear(qwin)
    blocks.clear(swin)
    seconds = reduce_second(group, own, mine, rbuf1, sbuf2, rbuf2, s2, r2, firsts)
    fetch.wait()

    def finish(ch, dst):
        sl = slice(ch * rows, (ch + 1) * rows)
        stream = (
            res_buf[sl].astype(F32)
            + mine[1, sl].astype(F32)
            + rbuf1[1, sl].astype(F32)
            + rbuf2[ch].astype(F32)
        )
        centered = stream - jnp.mean(stream, axis=1, keepdims=True)
        sigma = jnp.sqrt(jnp.mean(centered * centered, axis=1, keepdims=True) + epsilon)
        unit = centered / sigma
        unit_ref[sl] = unit
        sigma_ref[sl] = jnp.broadcast_to(sigma, (rows, 128))
        dst[...] = (unit * gain_ref[...]).astype(BF16)

    tails = spread(group, own, full, finish, seconds, ags, agr)
    up_load.wait()
    half = 2 * own

    @pl.loop(0, full.shape[0] // half)
    def _(b):
        span = pl.ds(pl.multiple_of(b * half, half), half)
        hidden = dot_nn(full[span, :], up_buf[...])
        copies = dot_nn(hidden.astype(BF16), pick_ref[...]) * cg_ref[...]
        act_src, slope_src = gelu_slope(hidden)
        act_copy, slope_copy = gelu_slope(copies)
        summed = act_src + dot_nt(act_copy.astype(BF16), pick_ref[...])
        merged_ref[span, :] = (summed * inv_ref[...]).astype(BF16)
        scaled = gm_ref[span, :] * inv_ref[...]
        grad_copy = dot_nn(scaled.astype(BF16), pick_ref[...]) * slope_copy * cg_ref[...]
        gh_ref[span, :] = (
            scaled * slope_src + dot_nt(grad_copy.astype(BF16), pick_ref[...])
        ).astype(BF16)

    for copy in firsts + seconds + tails:
        copy.wait_send()
    for index in range(4):
        blocks.arrive(q_ref, qwin, qs, qr, index)
        blocks.arrive(stat_ref, swin, ss, sr, index)
    blocks.left(q_ref, qwin, qs, qr)
    blocks.left(stat_ref, swin, ss, sr)


def reduce_scratch(own, width):
    two = VM((2, own, width), BF16)
    chunk = VM((CHUNKS, own // CHUNKS, width), BF16)
    return [two, two, two, chunk, chunk]


def reduce_sems():
    dma = pltpu.SemaphoreType.DMA
    return [dma((2,)), dma((2,)), dma((CHUNKS,)), dma((CHUNKS,))]


def norm_stage(count, groups, att, w, residual, gain, q, stats, up, pick, gm, inverse, copy_gain):
    tok, width = residual.shape
    own = tok // groups
    dma = pltpu.SemaphoreType.DMA
    vm = pl.BlockSpec(memory_space=VM)
    far = pl.BlockSpec(memory_space=pl.ANY)
    return pl.pallas_call(
        functools.partial(norm_kernel, count),
        out_shape=(
            jax.ShapeDtypeStruct(gm.shape, BF16),
            jax.ShapeDtypeStruct(gm.shape, BF16),
            jax.ShapeDtypeStruct((own, width), F32),
            jax.ShapeDtypeStruct((own, 128), F32),
            jax.ShapeDtypeStruct((4,) + q.shape, BF16),
            jax.ShapeDtypeStruct((4,) + stats.shape, F32),
        ),
        in_specs=[vm, vm, far, vm, vm, vm, far, vm, vm, vm, vm],
        out_specs=(vm,) * 6,
        scratch_shapes=reduce_scratch(own, width)
        + [VM((own, width), BF16), VM((tok, width), BF16), VM(up.shape, BF16)]
        + reduce_sems()
        + [dma((CHUNKS, 3)), dma((CHUNKS, 3))]
        + [dma((4,))] * 4
        + [dma(())] * 2,
        compiler_params=pltpu.CompilerParams(
            collective_id=2, has_side_effects=True, vmem_limit_bytes=48 << 20
        ),
        name="norm_stage",
    )(att, w, residual, gain, q, stats, up, pick, gm, inverse, copy_gain)


def back_kernel(
    gh_ref, up_ref, merged_ref, down_ref, cot_ref, gain_ref, unit_ref, sigma_ref,
    full, ffn_ref,
    mine, sbuf1, rbuf1, sbuf2, rbuf2, cot_buf, w_ref, down_buf,
    s1, r1, s2, r2, ags, agr, cot_sem, up_sem, down_sem,
):
    group = Group()
    own, width = unit_ref.shape
    rows = own // CHUNKS
    tiles = width // TILE

    def up_load(ct):
        span = pl.ds(pl.multiple_of(ct * TILE, TILE), TILE)
        return pltpu.make_async_copy(up_ref.at[span], w_ref.at[span], up_sem.at[ct])

    def down_load(ct):
        span = pl.ds(pl.multiple_of(ct * TILE, TILE), TILE)
        return pltpu.make_async_copy(down_ref.at[:, span], down_buf.at[ct], down_sem.at[ct])

    for ct in range(tiles):
        up_load(ct).start()
    fetch = pltpu.make_async_copy(
        cot_ref.at[pl.ds(pl.multiple_of(group.me * own, own), own)], cot_buf, cot_sem
    )
    fetch.start()
    barrier = pltpu.get_barrier_semaphore()
    group.greet(barrier)
    pl.semaphore_wait(barrier, 2)

    def part(owners, dst):
        lhs = jnp.concatenate(
            [gh_ref[pl.ds(pl.multiple_of(o * own, own), own), :] for o in owners], axis=0
        )

        @pl.loop(0, tiles)
        def _(ct):
            if dst is sbuf1:
                up_load(ct).wait()
            cols = pl.ds(pl.multiple_of(ct * TILE, TILE), TILE)
            r = dot_nt(lhs, w_ref[cols, :]).astype(BF16)
            dst[0, :, cols] = r[:own]
            dst[1, :, cols] = r[own:]

    for ct in range(tiles):
        down_load(ct).start()
    firsts = reduce_first(group, own, part, mine, sbuf1, rbuf1, s1, r1)
    seconds = reduce_second(group, own, mine, rbuf1, sbuf2, rbuf2, s2, r2, firsts)
    fetch.wait()

    @pl.loop(0, tiles)
    def _(ct):
        down_load(ct).wait()
        cols = pl.ds(pl.multiple_of(ct * TILE, TILE), TILE)
        ffn_ref[:, cols] = dot_nn(merged_ref[...], down_buf[ct]).astype(BF16)

    def finish(ch, dst):
        sl = slice(ch * rows, (ch + 1) * rows)
        grad = (
            cot_buf[sl].astype(F32)
            + mine[1, sl].astype(F32)
            + rbuf1[1, sl].astype(F32)
            + rbuf2[ch].astype(F32)
        )
        scaled = grad * gain_ref[...]
        unit = unit_ref[sl]
        mean = jnp.mean(scaled, axis=1, keepdims=True)
        along = jnp.mean(scaled * unit, axis=1, keepdims=True)
        dst[...] = ((scaled - mean - unit * along) / sigma_ref[sl, :1]).astype(BF16)

    tails = spread(group, own, full, finish, seconds, ags, agr)
    for copy in firsts + seconds + tails:
        copy.wait_send()


def back_stage(groups, gh, up, merged, down, cotangent, gain, unit, sigma):
    tok, width = cotangent.shape
    own = tok // groups
    dma = pltpu.SemaphoreType.DMA
    vm = pl.BlockSpec(memory_space=VM)
    far = pl.BlockSpec(memory_space=pl.ANY)
    tiles = width // TILE
    return pl.pallas_call(
        back_kernel,
        out_shape=(jax.ShapeDtypeStruct((tok, width), BF16),) * 2,
        in_specs=[vm, far, vm, far, far, vm, vm, vm],
        out_specs=(vm, vm),
        scratch_shapes=reduce_scratch(own, width)
        + [VM((own, width), BF16), VM(up.shape, BF16), VM((tiles, down.shape[0], TILE), BF16)]
        + reduce_sems()
        + [dma((CHUNKS, 3)), dma((CHUNKS, 3)), dma(()), dma((tiles,)), dma((tiles,))],
        compiler_params=pltpu.CompilerParams(
            collective_id=3, has_side_effects=True, vmem_limit_bytes=48 << 20
        ),
        name="back_stage",
    )(gh, up, merged, down, cotangent, gain, unit, sigma)


def grads_kernel(
    count, low_ref, w_ref, att_ref, q_ref, k_ref, v_ref, kwin, vwin, qwin, stat_ref, swin,
    ffn_ref, unit_ref, gain_ref,
    enc_ref, gq_ref, gk_ref, gv_ref,
    dwin, twin, do_ref, delta_ref, rbuf1, sbuf2, rbuf2,
    ds_, dr, ts, tr, s1, r1, s2, r2,
):
    blocks, group = Blocks(count), Group()
    own, width = unit_ref.shape
    tok, cols_all = q_ref.shape
    heads = cols_all // HEAD_DIM
    rows = own // CHUNKS
    barrier = pltpu.get_barrier_semaphore()
    group.greet(barrier)
    blocks.greet(barrier)
    blocks.greeted(barrier, 2)

    def ffn_rows(owner):
        return ffn_ref.at[pl.ds(pl.multiple_of(owner * own, own), own)]

    firsts = [
        remote(ffn_rows(owner), rbuf1.at[i], s1.at[i], r1.at[i], tp=group.sibling)
        for i, owner in enumerate((group.across, group.sibling))
    ]
    for copy in firsts:
        copy.start()
    lane = lax.broadcasted_iota(jnp.int32, (tok, 128), 1)
    grad_att = dot_nt(low_ref[...], w_ref[...]).astype(BF16)
    do_ref[...] = grad_att
    blocks.send(do_ref, dwin, ds_, dr)
    deltas = jnp.zeros((tok, 128), F32)
    for h in range(heads):
        cols = slice(h * HEAD_DIM, (h + 1) * HEAD_DIM)
        delta = jnp.sum(
            grad_att[:, cols].astype(F32) * att_ref[:, cols].astype(F32), axis=1, keepdims=True
        )
        deltas = jnp.where(lane == h, delta, deltas)
    delta_ref[...] = jnp.transpose(deltas)[:8]
    blocks.send(delta_ref, twin, ts, tr)
    blocks.clear(dwin)
    blocks.clear(twin)
    firsts[0].wait_recv()
    seconds = []
    far_rows = ffn_rows(group.far)
    for ch in range(CHUNKS):
        sl = slice(ch * rows, (ch + 1) * rows)
        sbuf2[ch] = (far_rows[sl].astype(F32) + rbuf1[0, sl].astype(F32)).astype(BF16)
        seconds.append(remote(sbuf2.at[ch], rbuf2.at[ch], s2.at[ch], r2.at[ch], tp=group.far))
        seconds[ch].start()

    def pair(queries, keys, values, grads, stats, delta_row, h):
        top = stats[pl.ds(h, 1), :]
        inverse = stats[pl.ds(heads + h, 1), :]
        prob = jnp.exp(dot_nt(keys, queries) * SCALE - top) * inverse
        slope = (prob * (dot_nt(values, grads) - delta_row[pl.ds(h, 1), :])).astype(BF16)
        return prob.astype(BF16), slope

    @pl.loop(0, heads)
    def _(h):
        cols = pl.ds(pl.multiple_of(h * HEAD_DIM, HEAD_DIM), HEAD_DIM)
        qh, gh = q_ref[:, cols], do_ref[:, cols]
        kh, vh = k_ref[:, cols], v_ref[:, cols]
        prob, slope = pair(qh, kh, vh, gh, stat_ref, delta_ref, h)
        gv_ref[:, cols] = dot_nn(prob, gh)
        gk_ref[:, cols] = dot_nn(slope, qh)
        acc = dot_tn(slope, kh)
        for index in range(4):
            k_off, v_off = kwin[index, :, cols], vwin[index, :, cols]
            live = jnp.where(blocks.there(OFFSETS[index]), 1.0, 0.0).astype(F32)
            _, slope = pair_off(qh, k_off, v_off, gh, stat_ref, delta_ref, h, live)
            acc = acc + dot_tn(slope, k_off)
        gq_ref[:, cols] = acc * SCALE

    for index in range(4):
        blocks.arrive(do_ref, dwin, ds_, dr, index)
        blocks.arrive(delta_ref, twin, ts, tr, index)

        @pl.when(blocks.there(OFFSETS[index]))
        def _():
            @pl.loop(0, heads)
            def _(h):
                cols = pl.ds(pl.multiple_of(h * HEAD_DIM, HEAD_DIM), HEAD_DIM)
                kh, vh = k_ref[:, cols], v_ref[:, cols]
                q_off, g_off = qwin[index, :, cols], dwin[index, :, cols]
                prob, slope = pair(q_off, kh, vh, g_off, swin.at[index], twin.at[index], h)
                gv_ref[:, cols] += dot_nn(prob, g_off)
                gk_ref[:, cols] += dot_nn(slope, q_off)

    gk_ref[...] = gk_ref[...] * SCALE

    firsts[1].wait_recv()
    near_rows = ffn_rows(group.me)
    for ch in range(CHUNKS):
        sl = slice(ch * rows, (ch + 1) * rows)
        seconds[ch].wait_recv()
        enc_ref[sl] = unit_ref[sl] * gain_ref[...] + (
            near_rows[sl].astype(F32) + rbuf1[1, sl].astype(F32) + rbuf2[ch].astype(F32)
        )
    for copy in firsts + seconds:
        copy.wait_send()
    blocks.left(do_ref, dwin, ds_, dr)
    blocks.left(delta_ref, twin, ts, tr)


def pair_off(queries, keys, values, grads, stats, delta_row, h, live):
    heads = stats.shape[0] // 2
    bias = (live - 1.0) * 1e30
    prob = jnp.exp(dot_nt(keys, queries) * SCALE + bias - stats[pl.ds(h, 1), :])
    prob = prob * stats[pl.ds(heads + h, 1), :]
    slope = (prob * (dot_nt(values, grads) - delta_row[pl.ds(h, 1), :])).astype(BF16)
    return None, slope


def grads_stage(count, low, w, att, q, k, v, kwin, vwin, qwin, stats, swin, ffn, unit, gain):
    tok, width = low.shape
    own = unit.shape[0]
    dma = pltpu.SemaphoreType.DMA
    vm = pl.BlockSpec(memory_space=VM)
    chunk = VM((CHUNKS, own // CHUNKS, width), BF16)
    grad = jax.ShapeDtypeStruct(q.shape, F32)
    return pl.pallas_call(
        functools.partial(grads_kernel, count),
        out_shape=(jax.ShapeDtypeStruct((own, width), F32), grad, grad, grad),
        in_specs=[vm] * 14,
        out_specs=(vm,) * 4,
        scratch_shapes=[
            VM((4,) + q.shape, BF16),
            VM((4, 8, tok), F32),
            VM(q.shape, BF16),
            VM((8, tok), F32),
            VM((2, own, width), BF16),
            chunk,
            chunk,
        ]
        + [dma((4,))] * 4
        + reduce_sems(),
        compiler_params=pltpu.CompilerParams(
            collective_id=4, has_side_effects=True, vmem_limit_bytes=48 << 20
        ),
        name="grads_stage",
    )(low, w, att, q, k, v, kwin, vwin, qwin, stats, swin, ffn, unit, gain)


def gelu_slope(v):
    rate = math.sqrt(2.0 / math.pi)
    square = v * v
    bend = jnp.tanh(rate * v * (1.0 + 0.044715 * square))
    level = 0.5 * (1.0 + bend)
    slope = level + (0.5 * rate) * v * (1.0 - bend * bend) * (1.0 + 0.134145 * square)
    return v * level, slope


def shards(
    count,
    groups,
    query_heads,
    key_heads,
    value_heads,
    residual,
    out_weight,
    ln_gain,
    up_source,
    down_source,
    copy_gain,
    neuron_source,
    cotangent,
):
    model_width = residual.shape[1]
    tp_place = lax.axis_index("tp")
    gain = ln_gain[None, :]
    src_width = up_source.shape[1]
    local_source = neuron_source - tp_place * src_width
    pick = (
        lax.broadcasted_iota(jnp.int32, (src_width, local_source.shape[0]), 0)
        == local_source[None, :]
    )
    counts = 1.0 + jnp.sum(pick.astype(F32), axis=1)
    inverse = 1.0 / counts
    pick = pick.astype(BF16)

    attended, kwin, vwin, stats, grad_merged = attend(
        count, query_heads, key_heads, value_heads, cotangent, down_source
    )
    merged, grad_hidden, unit, sigma, qwin, swin = norm_stage(
        count, groups, attended, out_weight, residual, gain, query_heads, stats,
        up_source, pick, grad_merged, inverse[None, :], copy_gain[None, :],
    )
    grad_low, ffn_part = back_stage(
        groups, grad_hidden, up_source, merged, down_source, cotangent, gain, unit, sigma
    )
    encoded, grad_query, grad_key, grad_value = grads_stage(
        count, grad_low, out_weight, attended, query_heads, key_heads, value_heads,
        kwin, vwin, qwin, stats, swin, ffn_part, unit, gain,
    )
    col_width = model_width // groups
    grad_residual = lax.dynamic_slice_in_dim(grad_low, tp_place * col_width, col_width, 1)
    return (encoded, grad_query, grad_key, grad_value, grad_residual.astype(F32))


def solution(mesh):
    in_specs = (
        P("seq", "tp"),
        P("seq", "tp"),
        P("seq", "tp"),
        P("seq", None),
        P("tp", None),
        P(),
        P(None, "tp"),
        P("tp", None),
        P("tp"),
        P("tp"),
        P("seq", None),
    )
    out_specs = (
        P(("seq", "tp"), None),
        P("seq", "tp"),
        P("seq", "tp"),
        P("seq", "tp"),
        P("seq", "tp"),
    )
    body = functools.partial(shards, mesh.shape["seq"], mesh.shape["tp"])
    return jax.shard_map(body, mesh=mesh, in_specs=in_specs, out_specs=out_specs, check_vma=False)
```
